32 devices in a mesh: row: 2 (over y), col: 8 (over z, x), rep: 2 (over core).
Axes of the slice: x: 2, y: 2, z: 4, core: 2. Of those that a mesh axis runs over, the one named last changes fastest.
Arguments:
- ancestor_inverse: float32 [2048, 2048], P('row', 'col'), may hold values from -6 to 6
- tile_structure: int32 [16, 16], P('row', 'col'), may hold values from 0 to 1, as said below
- factor: float32 [2048, 512], P(('row', 'col')), may hold values from -0.125 to 0.125
- factor_normalizer: float32 [512, 512], replicated, may hold values from -1 to 1, as said below
- pivot_inverse: float32 [512, 512], P(None, 'rep'), may hold values from -6 to 6, as said below
Outputs:
- ancestor_columns: float32 [2048, 512], P(('row', 'col'), 'rep')
- diag_block: float32 [512, 512], P(None, 'rep')
The draws below stay inside these ranges and needn't reach their ends.
Inputs may be any that keep to these rules, and one draw needn't show every extreme that they name: `tile_structure`: symmetric, with ones on the diagonal. `factor_normalizer`: lower triangular with ones on its diagonal. `pivot_inverse`: symmetric.
All inputs are finite; a program needn't handle non-finite values.
Results may differ from the reference program's by a relative error of at most 0.000078.
Values sent between devices are 32-bit elements; how exact they have to be, the bound alone decides.
No kernel may reach another device: no remote copies, remote signals or barrier semaphores. Data moves between devices by JAX's collectives and lax.ppermute only.
A program may use at most 64 MiB of HBM per device.

```python
import jax
import jax.numpy as jnp
from jax import lax

WIDTH = 512
TILE = 128
TILES = 16
ROWS = 2048


def draw_tile_structure(key, part):
    raw_bits = jax.random.randint(key, (TILES, TILES), 0, 2, dtype=jnp.int32)
    upper_part = jnp.triu(raw_bits, 1)
    return upper_part + upper_part.T + jnp.eye(TILES, dtype=jnp.int32)


def draw_factor_normalizer(key, part):
    inner_key = jax.random.fold_in(key, 11)
    entries = jnp.clip(jax.random.normal(inner_key, (WIDTH, WIDTH), jnp.float32), -4.0, 4.0)
    lower_part = jnp.tril(entries, -1) * (0.8 / jnp.sqrt(jnp.float32(WIDTH)))
    return lower_part + jnp.eye(WIDTH, dtype=jnp.float32)


def draw_pivot_inverse(key, part):
    inner_key = jax.random.fold_in(key, 23)
    entries = jnp.clip(jax.random.normal(inner_key, (WIDTH, WIDTH), jnp.float32), -4.0, 4.0)
    return (entries + entries.T) * 0.7071


def steps_of(own_key, dims, shards, low, largest):
    gain, own = 1.0, jax.random.fold_in(own_key, 6)
    for position, parts in shards:
        heights = jnp.exp(jax.random.uniform(jax.random.fold_in(own, position), (parts,), jnp.float32, low / len(shards), largest / len(shards)))
        gain = gain * jnp.repeat(heights, dims[position] // parts).reshape([-1 if axis == position else 1 for axis in range(len(dims))])
    return gain


def centred(own_key, shape, deviation, bound, cuts=(), held_as=jnp.bfloat16):
    gain = steps_of(own_key, shape, cuts, -0.22, 0.18) if cuts else 1.0
    array = jax.random.normal(own_key, shape, jnp.float32) * deviation * gain
    return jnp.minimum(jnp.maximum(array, -bound), bound).astype(held_as)


def setup_inputs(seed: int = 0) -> dict:
    keys = jax.random.split(jax.random.key(seed), 6)
    ancestor_inverse = centred(keys[0], (ROWS, ROWS), 1.0, 6.0, ((0, 2), (1, 8)), jnp.float32)
    tile_structure = draw_tile_structure(jax.random.fold_in(keys[5], 71), 0)
    factor = centred(keys[2], (ROWS, WIDTH), ROWS ** -0.5, 0.125, ((0, 16),), jnp.float32)
    factor_normalizer = draw_factor_normalizer(jax.random.fold_in(keys[5], 71), 0)
    pivot_inverse = draw_pivot_inverse(jax.random.fold_in(keys[5], 71), 0)
    return {"ancestor_inverse": ancestor_inverse, "tile_structure": tile_structure, "factor": factor, "factor_normalizer": factor_normalizer, "pivot_inverse": pivot_inverse}


def reference(ancestor_inverse, tile_structure, factor, factor_normalizer, pivot_inverse):
    normed = jnp.dot(factor, factor_normalizer, precision=lax.Precision.HIGHEST, preferred_element_type=jnp.float32)

    def one_tile(index):
        inverse_rows = lax.dynamic_slice_in_dim(ancestor_inverse, index * TILE, TILE, 0)
        tile_marks = lax.dynamic_slice_in_dim(tile_structure, index, 1, 0).astype(jnp.float32)
        masked = (inverse_rows.reshape(TILE, TILES, TILE) * tile_marks.reshape(1, TILES, 1)).reshape(TILE, ROWS)
        return -jnp.dot(masked, normed, precision=lax.Precision.HIGHEST, preferred_element_type=jnp.float32)

    ancestor_columns = lax.map(one_tile, jnp.arange(TILES, dtype=jnp.int32)).reshape(ROWS, WIDTH)
    coupling = lax.dot_general(normed, ancestor_columns, (((0,), (0,)), ((), ())), precision=lax.Precision.HIGHEST, preferred_element_type=jnp.float32)
    diag_block = pivot_inverse - 0.5 * (coupling + coupling.T)
    return ancestor_columns, diag_block
```

```python
import jax
import jax.numpy as jnp
from jax import lax
from jax.sharding import PartitionSpec as P

AXES = ("row", "col", "rep")
PAIR = 2


def send(block, target):
    rows, cols, reps = (lax.axis_size(name) for name in AXES)

    def flat(r, c, p):
        return (r * cols + c) * reps + p

    route = [
        (flat(r, c, p), flat(*target(r, c, p)))
        for r in range(rows)
        for c in range(cols)
        for p in range(reps)
    ]
    return lax.ppermute(block, AXES, route)


def dot(left, right, contract=(1, 0)):
    return lax.dot_general(
        left,
        right,
        (((contract[0],), (contract[1],)), ((), ())),
        precision=lax.Precision.HIGH,
        preferred_element_type=jnp.float32,
    )


def swap_core(block):
    return send(block, lambda r, c, p: (r, c, 1 - p))


def body(ancestor_inverse, tile_structure, factor, factor_normalizer, pivot_inverse):
    tile = factor.shape[0]
    half = pivot_inverse.shape[1]
    rows, cols = lax.axis_size("row"), lax.axis_size("col")
    row, col, rep = (lax.axis_index(name) for name in AXES)

    normed = dot(factor, factor_normalizer)
    own_normed = lax.dynamic_slice_in_dim(normed, rep * half, half, 1)

    def to_column(k):
        def target(r, c, p):
            block = r * cols + c
            return (block % rows) ^ k, block // rows, p

        return target

    arrived = [send(own_normed, to_column(k)) for k in range(rows)]
    column_block = jnp.stack(arrived)[jnp.arange(rows) ^ row].reshape(rows * tile, half)

    marks = tile_structure.astype(jnp.float32)
    masked = (
        ancestor_inverse.reshape(cols, tile, rows, tile) * marks[:, None, :, None]
    ).reshape(cols, tile, rows * tile)
    order = jnp.arange(cols) ^ col
    product = dot(masked[order].reshape(cols * tile, rows * tile), column_block)
    product = product.reshape(cols, tile, half)
    shares = [product[0]] + [
        send(product[k], lambda r, c, p, k=k: (r, c ^ k, p)) for k in range(1, cols)
    ]
    ancestor_columns = -sum(shares)

    other_columns = swap_core(ancestor_columns)
    other_normed = lax.dynamic_slice_in_dim(normed, (1 - rep) * half, half, 1)
    first = rep == 0
    quarter = half // 2

    def stacked(top, bottom):
        return jnp.concatenate([top, bottom], 0)

    def right_part(own, other):
        return jnp.where(first, other[:, :quarter], own[:, quarter:])

    diagonal = dot(stacked(own_normed, ancestor_columns), stacked(ancestor_columns, own_normed), (0, 0))
    left_side = stacked(
        jnp.where(first, own_normed, other_normed),
        jnp.where(first, ancestor_columns, other_columns),
    )
    right_side = stacked(
        right_part(ancestor_columns, other_columns), right_part(own_normed, other_normed)
    )
    between = dot(left_side, right_side, (0, 0))
    total = jnp.concatenate([diagonal, between], 1)

    members = rows * PAIR
    place = row * PAIR + col % PAIR
    width = half + quarter
    step = half // members

    def in_plane(k):
        def target(r, c, p):
            peer = (r * PAIR + c % PAIR) ^ k
            return peer // PAIR, c // PAIR * PAIR + peer % PAIR, p

        return target

    parts = total.reshape(members, step, width)
    parts = parts[jnp.arange(members) ^ place]
    part = parts[0] + sum(send(parts[k], in_plane(k)) for k in range(1, members))
    part = part + sum(
        send(part, lambda r, c, p, k=k: (r, c ^ (k * PAIR), p)) for k in range(1, cols // PAIR)
    )
    gathered = jnp.stack([part] + [send(part, in_plane(k)) for k in range(1, members)])
    total = gathered[jnp.arange(members) ^ place].reshape(half, width)
    diagonal, between = total[:, :half], total[:, half:]
    other_between = swap_core(between)
    across = jnp.where(
        first,
        jnp.concatenate([between, other_between], 1),
        jnp.concatenate([other_between, between], 1),
    )
    symmetric = jnp.where(
        first,
        jnp.concatenate([diagonal, across.T], 0),
        jnp.concatenate([across, diagonal], 0),
    )
    return ancestor_columns, pivot_inverse - 0.5 * symmetric


def solution(mesh):
    return jax.shard_map(
        body,
        mesh=mesh,
        in_specs=(P("row", "col"), P("row", "col"), P(("row", "col"), None), P(), P(None, "rep")),
        out_specs=(P(("row", "col"), "rep"), P(None, "rep")),
        check_vma=False,
    )
```

```python
import functools

import jax
import jax.numpy as jnp
from jax import lax
from jax.experimental import pallas as pl
from jax.experimental.pallas import tpu as pltpu
from jax.sharding import PartitionSpec as P


AXES = ("row", "col", "rep")
PAIR = 2
F32, BF16 = jnp.float32, jnp.bfloat16


def send(block, target):
    rows, cols, reps = (lax.axis_size(axis) for axis in AXES)

    def flat(r, c, p):
        return (r * cols + c) * reps + p

    route = [
        (flat(r, c, p), flat(*target(r, c, p)))
        for r in range(rows)
        for c in range(cols)
        for p in range(reps)
    ]
    return lax.ppermute(block, AXES, route)


def swap_core(block):
    return send(block, lambda r, c, p: (r, c, 1 - p))


def dot(left, right):
    return jnp.dot(left, right, precision=lax.Precision.HIGH, preferred_element_type=F32)


def split(value):
    high = value.astype(BF16)
    return high, (value - high.astype(F32)).astype(BF16)


def split_dot(left, right, contract=(1, 0)):
    dims = (((contract[0],), (contract[1],)), ((), ()))
    product = functools.partial(
        lax.dot_general, dimension_numbers=dims, preferred_element_type=F32
    )
    return (
        product(left[0], right[1]) + product(left[1], right[0]) + product(left[0], right[0])
    )


def tile_at(index, size):
    return pl.ds(pl.multiple_of(index * size, size), size)


def prepare_kernel(planes, rows, tile, place_ref, marks_ref, full_ref, kept_ref, given_ref):
    row, plane, side, rep = (place_ref[i] for i in range(4))
    cut = planes // 2

    def masked(k, wanted, m):
        source, across = (plane ^ k) * PAIR + wanted, row ^ m
        mark = marks_ref[source, across].astype(F32)
        return full_ref[tile_at(source, tile), tile_at(across, tile)] * mark

    for m in range(rows):
        columns = pl.ds(m * tile, tile)

        @pl.loop(0, cut)
        def _(k):
            given_ref[k, :, columns] = masked(k + rep * cut, 1 - side, m)

        @pl.loop(0, planes)
        def _(k):
            kept_ref[k, :, columns] = masked(k, side, m)


def product_kernel(planes, members, place_ref, kept_ref, mine_ref, theirs_ref, *refs):
    arrived, outs = refs[:members], refs[members:]
    cut = planes // 2
    rep = place_ref[3]
    right = split(jnp.concatenate([ref[...] for ref in arrived], 0))
    for k in range(planes):
        taken = jnp.where(rep == k // cut, mine_ref[k % cut], theirs_ref[k % cut])
        left = jnp.concatenate([kept_ref[k], taken], 1)
        outs[k][...] = split_dot(split(left), right)


def coupling_kernel(members, place_ref, normed_ref, other_normed_ref, columns_ref, other_ref, *refs):
    outs, total_ref = refs[:members], refs[members]
    place, first = place_ref[4], place_ref[3] == 0
    half = normed_ref.shape[1]
    quarter, step = half // 2, half // members
    own_normed, own = normed_ref[...], columns_ref[...]
    other_normed, other = other_normed_ref[...], other_ref[...]
    mixed = split_dot(split(own_normed), split(own), (0, 0))
    total_ref[:, :half] = mixed + mixed.T

    def left(mine, theirs):
        return split(jnp.where(first, mine, theirs))

    def right(mine, theirs):
        return split(jnp.where(first, theirs[:, :quarter], mine[:, quarter:]))

    total_ref[:, half:] = split_dot(
        left(own_normed, other_normed), right(own, other), (0, 0)
    ) + split_dot(left(own, other), right(own_normed, other_normed), (0, 0))
    for k in range(members):
        outs[k][...] = total_ref[tile_at(place ^ k, step), :]


def finish_kernel(members, place_ref, pivot_ref, other_ref, *refs):
    parts, out_ref, total_ref, between_ref = refs[:members], *refs[members:]
    place, rep = place_ref[4], place_ref[3]
    half = out_ref.shape[1]
    step = half // members
    for k in range(members):
        rows = tile_at(place ^ k, step)
        total_ref[rows, :] = parts[k][...]
        between_ref[rows, :] = other_ref[k * step : (k + 1) * step, :]

    @pl.when(rep == 0)
    def _():
        across = jnp.concatenate([total_ref[:, half:], between_ref[...]], 1)
        out_ref[:half, :] = pivot_ref[:half, :] - 0.5 * total_ref[:, :half]
        out_ref[half:, :] = pivot_ref[half:, :] - 0.5 * across.T

    @pl.when(rep != 0)
    def _():
        across = jnp.concatenate([between_ref[...], total_ref[:, half:]], 1)
        out_ref[:half, :] = pivot_ref[:half, :] - 0.5 * across
        out_ref[half:, :] = pivot_ref[half:, :] - 0.5 * total_ref[:, :half]


def call(kernel, shapes, in_smem, args, scratch=(), flops=0):
    smem, vmem = pl.BlockSpec(memory_space=pltpu.SMEM), pl.BlockSpec(memory_space=pltpu.VMEM)
    moved = sum(4 * a.size for a in args) + sum(4 * functools.reduce(int.__mul__, s) for s in shapes)
    return pl.pallas_call(
        kernel,
        out_shape=[jax.ShapeDtypeStruct(shape, F32) for shape in shapes],
        in_specs=[smem] * in_smem + [vmem] * (len(args) - in_smem),
        out_specs=[vmem] * len(shapes),
        scratch_shapes=[pltpu.VMEM(shape, F32) for shape in scratch],
        compiler_params=pltpu.CompilerParams(vmem_limit_bytes=3 * moved + 2**21),
        cost_estimate=pl.CostEstimate(flops=flops, bytes_accessed=moved, transcendentals=0),
    )(*args)


def body(ancestor_inverse, tile_structure, factor, factor_normalizer, pivot_inverse):
    tile = factor.shape[0]
    half = pivot_inverse.shape[1]
    rows, cols = lax.axis_size("row"), lax.axis_size("col")
    row, col, rep = (lax.axis_index(name) for name in AXES)
    planes, members = cols // PAIR, rows * PAIR
    plane, side = col // PAIR, col % PAIR
    place = jnp.stack([row, plane, side, rep, row * PAIR + side]).astype(jnp.int32)
    depth = rows * tile

    def half_of(matrix, index):
        return lax.dynamic_slice_in_dim(matrix, index * half, half, 1)

    own_normed = dot(factor, half_of(factor_normalizer, rep))

    def to_plane(k):
        def target(r, c, p):
            block = r * cols + c
            peer = (block % members) ^ k
            return peer % rows, block // members * PAIR + peer // rows, p

        return target

    arrived = [send(own_normed, to_plane(k)) for k in range(members)]
    other_normed = dot(factor, half_of(factor_normalizer, 1 - rep))

    cut = planes // 2
    kept, given = call(
        functools.partial(prepare_kernel, planes, rows, tile),
        [(planes, tile, depth), (cut, tile, depth)],
        2,
        [place, tile_structure, ancestor_inverse],
    )
    mine = send(given, lambda r, c, p: (r, c ^ 1, p))
    theirs = swap_core(mine)
    shares = call(
        functools.partial(product_kernel, planes, members),
        [(tile, half)] * planes,
        1,
        [place, kept, mine, theirs, *arrived],
        flops=12 * planes * tile * depth * half,
    )
    ancestor_columns = -(
        shares[0]
        + sum(
            send(shares[k], lambda r, c, p, k=k: (r, c ^ (k * PAIR), p))
            for k in range(1, planes)
        )
    )

    other_columns = swap_core(ancestor_columns)
    quarter, step = half // 2, half // members
    width = half + quarter
    parts = call(
        functools.partial(coupling_kernel, members),
        [(step, width)] * members,
        1,
        [place, own_normed, other_normed, ancestor_columns, other_columns],
        [(half, width)],
        flops=12 * tile * half * half,
    )

    def in_plane(k):
        def target(r, c, p):
            peer = (r * PAIR + c % PAIR) ^ k
            return peer // PAIR, c // PAIR * PAIR + peer % PAIR, p

        return target

    part = parts[0] + sum(send(parts[k], in_plane(k)) for k in range(1, members))
    part = part + sum(
        send(part, lambda r, c, p, k=k: (r, c ^ (k * PAIR), p))
        for k in range(1, planes)
    )
    parts = [part] + [send(part, in_plane(k)) for k in range(1, members)]
    other_between = swap_core(jnp.concatenate([one[:, half:] for one in parts], 0))
    (diag_block,) = call(
        functools.partial(finish_kernel, members),
        [pivot_inverse.shape],
        1,
        [place, pivot_inverse, other_between, *parts],
        [(half, width), (half, quarter)],
    )
    return ancestor_columns, diag_block


def solution(mesh):
    return jax.shard_map(
        body,
        mesh=mesh,
        in_specs=(P("row", "col"), P("row", "col"), P(("row", "col"), None), P(), P(None, "rep")),
        out_specs=(P(("row", "col"), "rep"), P(None, "rep")),
        check_vma=False,
    )
```

```python
import functools

import jax
import jax.numpy as jnp
from jax import lax
from jax.experimental import pallas as pl
from jax.experimental.pallas import tpu as pltpu
from jax.sharding import PartitionSpec as P


AXES = ("row", "col", "rep")
PAIR = 2
F32, BF16 = jnp.float32, jnp.bfloat16


def send(block, target):
    rows, cols, reps = (lax.axis_size(axis) for axis in AXES)

    def flat(r, c, p):
        return (r * cols + c) * reps + p

    route = [
        (flat(r, c, p), flat(*target(r, c, p)))
        for r in range(rows)
        for c in range(cols)
        for p in range(reps)
    ]
    return lax.ppermute(block, AXES, route)


def swap_core(block):
    return send(block, lambda r, c, p: (r, c, 1 - p))


def dot(left, right):
    return jnp.dot(left, right, precision=lax.Precision.HIGH, preferred_element_type=F32)


def split(value):
    high = value.astype(BF16)
    return high, (value - high.astype(F32)).astype(BF16)


def split_dot(left, right, contract=(1, 0)):
    dims = (((contract[0],), (contract[1],)), ((), ()))
    product = functools.partial(
        lax.dot_general, dimension_numbers=dims, preferred_element_type=F32
    )
    return (
        product(left[0], right[1]) + product(left[1], right[0]) + product(left[0], right[0])
    )


def tile_at(index, size):
    return pl.ds(pl.multiple_of(index * size, size), size)


def prepare_kernel(planes, rows, tile, place_ref, marks_ref, full_ref, kept_ref, given_ref):
    row, plane, side, rep = (place_ref[i] for i in range(4))
    cut = planes // 2

    def masked(k, wanted, m):
        source, across = (plane ^ k) * PAIR + wanted, row ^ m
        mark = marks_ref[source, across].astype(F32)
        return full_ref[tile_at(source, tile), tile_at(across, tile)] * mark

    for m in range(rows):
        columns = pl.ds(m * tile, tile)

        @pl.loop(0, cut)
        def _(k):
            given_ref[k, :, columns] = masked(k + rep * cut, 1 - side, m)

        @pl.loop(0, planes)
        def _(k):
            kept_ref[k, :, columns] = masked(k, side, m)


def product_kernel(planes, members, place_ref, kept_ref, mine_ref, theirs_ref, *refs):
    arrived, outs = refs[:members], refs[members:]
    cut = planes // 2
    rep = place_ref[3]
    right = split(jnp.concatenate([ref[...] for ref in arrived], 0))
    for k in range(planes):
        taken = jnp.where(rep == k // cut, mine_ref[k % cut], theirs_ref[k % cut])
        left = jnp.concatenate([kept_ref[k], taken], 1)
        share = split_dot(split(left), right)
        outs[0][k] = share
        if k:
            outs[k][...] = share


def coupling_kernel(members, planes, place_ref, share_ref, other_ref, gathered_ref, *refs):
    strip, outs, total_ref = refs[: planes + 1], refs[planes + 1 : -1], refs[-1]
    place, first = place_ref[4], place_ref[3] == 0
    tile, half = strip[0].shape
    quarter, step = half // 2, half // members
    own_normed = jnp.concatenate([ref[...] for ref in strip[:planes]], 0)
    other_normed = jnp.concatenate([strip[planes][...], gathered_ref[...]], 0)
    own = share_ref[...].reshape(planes * tile, half)
    other = other_ref[...].reshape(planes * tile, half)
    mixed = split_dot(split(own_normed), split(own), (0, 0))
    total_ref[:, :half] = mixed + mixed.T

    def left(mine, theirs):
        return split(jnp.where(first, mine, theirs))

    def right(mine, theirs):
        return split(jnp.where(first, theirs[:, :quarter], mine[:, quarter:]))

    total_ref[:, half:] = split_dot(
        left(own_normed, other_normed), right(own, other), (0, 0)
    ) + split_dot(left(own, other), right(own_normed, other_normed), (0, 0))
    for k in range(members):
        outs[k][...] = total_ref[tile_at(place ^ k, step), :]


def finish_kernel(members, place_ref, pivot_ref, other_ref, *refs):
    parts, out_ref, total_ref, between_ref = refs[:members], *refs[members:]
    place, rep = place_ref[4], place_ref[3]
    half = out_ref.shape[1]
    step = half // members
    for k in range(members):
        rows = tile_at(place ^ k, step)
        total_ref[rows, :] = parts[k][...]
        between_ref[rows, :] = other_ref[k * step : (k + 1) * step, :]

    @pl.when(rep == 0)
    def _():
        across = jnp.concatenate([total_ref[:, half:], between_ref[...]], 1)
        out_ref[:half, :] = pivot_ref[:half, :] + 0.5 * total_ref[:, :half]
        out_ref[half:, :] = pivot_ref[half:, :] + 0.5 * across.T

    @pl.when(rep != 0)
    def _():
        across = jnp.concatenate([between_ref[...], total_ref[:, half:]], 1)
        out_ref[:half, :] = pivot_ref[:half, :] + 0.5 * across
        out_ref[half:, :] = pivot_ref[half:, :] + 0.5 * total_ref[:, :half]


def call(kernel, shapes, in_smem, args, scratch=(), flops=0):
    smem, vmem = pl.BlockSpec(memory_space=pltpu.SMEM), pl.BlockSpec(memory_space=pltpu.VMEM)
    moved = sum(4 * a.size for a in args) + sum(4 * functools.reduce(int.__mul__, s) for s in shapes)
    return pl.pallas_call(
        kernel,
        out_shape=[jax.ShapeDtypeStruct(shape, F32) for shape in shapes],
        in_specs=[smem] * in_smem + [vmem] * (len(args) - in_smem),
        out_specs=[vmem] * len(shapes),
        scratch_shapes=[pltpu.VMEM(shape, F32) for shape in scratch],
        compiler_params=pltpu.CompilerParams(vmem_limit_bytes=3 * moved + 2**21),
        cost_estimate=pl.CostEstimate(flops=flops, bytes_accessed=moved, transcendentals=0),
    )(*args)


def body(ancestor_inverse, tile_structure, factor, factor_normalizer, pivot_inverse):
    tile = factor.shape[0]
    half = pivot_inverse.shape[1]
    rows, cols = lax.axis_size("row"), lax.axis_size("col")
    row, col, rep = (lax.axis_index(name) for name in AXES)
    planes, members = cols // PAIR, rows * PAIR
    plane, side = col // PAIR, col % PAIR
    place = jnp.stack([row, plane, side, rep, row * PAIR + side]).astype(jnp.int32)
    depth = rows * tile

    def half_of(matrix, index):
        return lax.dynamic_slice_in_dim(matrix, index * half, half, 1)

    own_normed = dot(factor, half_of(factor_normalizer, rep))

    def to_plane(r, c, p):
        block = r * cols + c
        peer = block % members
        return peer % rows, block // members * PAIR + peer // rows, p

    def beside(k):
        def target(r, c, p):
            peer = (c % PAIR * rows + r) ^ k
            return peer % rows, c // PAIR * PAIR + peer // rows, p

        return target

    def along(k):
        return lambda r, c, p: (r, c ^ (k * PAIR), p)

    arrived = [send(own_normed, to_plane)]
    arrived += [send(arrived[0], beside(k)) for k in range(1, members)]
    strip = [own_normed] + [send(own_normed, along(k)) for k in range(1, planes)]
    other_strip = swap_core(jnp.concatenate(strip[1:], 0))
    other_normed = dot(factor, half_of(factor_normalizer, 1 - rep))

    cut = planes // 2
    kept, given = call(
        functools.partial(prepare_kernel, planes, rows, tile),
        [(planes, tile, depth), (cut, tile, depth)],
        2,
        [place, tile_structure, ancestor_inverse],
    )
    mine = send(given, lambda r, c, p: (r, c ^ 1, p))
    theirs = swap_core(mine)
    product, *shares = call(
        functools.partial(product_kernel, planes, members),
        [(planes, tile, half)] + [(tile, half)] * (planes - 1),
        1,
        [place, kept, mine, theirs, *arrived],
        flops=12 * planes * tile * depth * half,
    )
    other_product = swap_core(product)
    ancestor_columns = -(product[0] + sum(send(shares[k - 1], along(k)) for k in range(1, planes)))

    quarter, step = half // 2, half // members
    width = half + quarter
    parts = call(
        functools.partial(coupling_kernel, members, planes),
        [(step, width)] * members,
        1,
        [place, product, other_product, other_strip, *strip, other_normed],
        [(half, width)],
        flops=12 * planes * tile * half * half,
    )

    def in_plane(k):
        def target(r, c, p):
            peer = (r * PAIR + c % PAIR) ^ k
            return peer // PAIR, c // PAIR * PAIR + peer % PAIR, p

        return target

    part = parts[0] + sum(send(parts[k], in_plane(k)) for k in range(1, members))
    part = part + sum(send(part, along(k)) for k in range(1, planes))
    parts = [part] + [send(part, in_plane(k)) for k in range(1, members)]
    other_between = swap_core(jnp.concatenate([one[:, half:] for one in parts], 0))
    (diag_block,) = call(
        functools.partial(finish_kernel, members),
        [pivot_inverse.shape],
        1,
        [place, pivot_inverse, other_between, *parts],
        [(half, width), (half, quarter)],
    )
    return ancestor_columns, diag_block


def solution(mesh):
    return jax.shard_map(
        body,
        mesh=mesh,
        in_specs=(P("row", "col"), P("row", "col"), P(("row", "col"), None), P(), P(None, "rep")),
        out_specs=(P(("row", "col"), "rep"), P(None, "rep")),
        check_vma=False,
    )
```

```python
import functools

import jax
import jax.numpy as jnp
from jax import lax
from jax.experimental import pallas as pl
from jax.experimental.pallas import tpu as pltpu
from jax.sharding import PartitionSpec as P


AXES = ("row", "col", "rep")
PAIR = 2
ROOM = 56000000
F32, BF16 = jnp.float32, jnp.bfloat16


def send(block, target):
    rows, cols, reps = (lax.axis_size(axis) for axis in AXES)

    def flat(r, c, p):
        return (r * cols + c) * reps + p

    route = [
        (flat(r, c, p), flat(*target(r, c, p)))
        for r in range(rows)
        for c in range(cols)
        for p in range(reps)
    ]
    return lax.ppermute(block, AXES, route)


def swap_core(block):
    return send(block, lambda r, c, p: (r, c, 1 - p))


def split(value):
    high = value.astype(BF16)
    return high, (value - high.astype(F32)).astype(BF16)


def split_dot(left, right, contract=(1, 0)):
    dims = (((contract[0],), (contract[1],)), ((), ()))
    product = functools.partial(
        lax.dot_general, dimension_numbers=dims, preferred_element_type=F32
    )
    return (
        product(left[0], right[1]) + product(left[1], right[0]) + product(left[0], right[0])
    )


def tile_at(index, size):
    return pl.ds(pl.multiple_of(index * size, size), size)


def front_kernel(planes, rows, place_ref, marks_ref, factor_ref, normalizer_ref, full_ref, *refs):
    normed_ref, other_ref, kept_ref, given_ref, *scratch = refs
    factor_in, normalizer_in, full_in, sems = scratch
    row, plane, side, rep = (place_ref[i] for i in range(4))
    tile, half = normed_ref.shape
    cut = planes // 2
    band = PAIR * tile
    loads = [
        pltpu.make_async_copy(factor_ref, factor_in, sems.at[0]),
    ] + [
        pltpu.make_async_copy(
            normalizer_ref.at[:, tile_at(columns, half)], normalizer_in.at[i], sems.at[1 + i]
        )
        for i, columns in enumerate((rep, 1 - rep))
    ] + [
        pltpu.make_async_copy(full_ref.at[tile_at(plane ^ k, band), :], full_in.at[k], sems.at[3 + k])
        for k in range(planes)
    ]
    for load in loads:
        load.start()
    for load in loads[:2]:
        load.wait()
    left = split(factor_in[...])
    normed_ref[...] = split_dot(left, split(normalizer_in[0]))
    for load in loads[2:]:
        load.wait()
    other_ref[...] = split_dot(left, split(normalizer_in[1]))

    def masked(k, wanted, m):
        across = row ^ m
        mark = marks_ref[across, (plane ^ k) * PAIR + wanted].astype(F32)
        return full_in[k, tile_at(wanted, tile), tile_at(across, tile)] * mark

    for m in range(rows):
        columns = pl.ds(m * tile, tile)

        @pl.loop(0, cut)
        def _(k):
            given_ref[k, :, columns] = masked(k + rep * cut, 1 - side, m)

        @pl.loop(0, planes)
        def _(k):
            kept_ref[k, :, columns] = masked(k, side, m)


def product_kernel(planes, members, place_ref, kept_ref, mine_ref, theirs_ref, *refs):
    arrived, outs = refs[:members], refs[members:]
    cut = planes // 2
    rep = place_ref[3]
    right = split(jnp.concatenate([ref[...] for ref in arrived], 0))
    for k in range(planes):
        taken = jnp.where(rep == k // cut, mine_ref[k % cut], theirs_ref[k % cut])
        left = jnp.concatenate([kept_ref[k], taken], 1)
        share = split_dot(split(left), right)
        outs[0][k] = share
        if k:
            outs[k][...] = share


def coupling_kernel(members, planes, place_ref, share_ref, other_ref, gathered_ref, *refs):
    strip, outs, total_ref = refs[: planes + 1], refs[planes + 1 : -1], refs[-1]
    place, first = place_ref[4], place_ref[3] == 0
    tile, half = strip[0].shape
    quarter, step = half // 2, half // members
    own_normed = jnp.concatenate([ref[...] for ref in strip[:planes]], 0)
    other_normed = jnp.concatenate([strip[planes][...], gathered_ref[...]], 0)
    own = share_ref[...].reshape(planes * tile, half)
    other = other_ref[...].reshape(planes * tile, half)
    mixed = split_dot(split(own_normed), split(own), (0, 0))
    total_ref[:, :half] = mixed + mixed.T

    def left(mine, theirs):
        return split(jnp.where(first, mine, theirs))

    def right(mine, theirs):
        return split(jnp.where(first, theirs[:, :quarter], mine[:, quarter:]))

    total_ref[:, half:] = split_dot(
        left(own_normed, other_normed), right(own, other), (0, 0)
    ) + split_dot(left(own, other), right(own_normed, other_normed), (0, 0))
    for k in range(members):
        outs[k][...] = total_ref[tile_at(place ^ k, step), :]


def finish_kernel(members, place_ref, pivot_ref, other_ref, *refs):
    parts, out_ref, total_ref, between_ref = refs[:members], *refs[members:]
    place, rep = place_ref[4], place_ref[3]
    half = out_ref.shape[1]
    step = half // members
    for k in range(members):
        rows = tile_at(place ^ k, step)
        total_ref[rows, :] = parts[k][...]
        between_ref[rows, :] = other_ref[k * step : (k + 1) * step, :]

    @pl.when(rep == 0)
    def _():
        across = jnp.concatenate([total_ref[:, half:], between_ref[...]], 1)
        out_ref[:half, :] = pivot_ref[:half, :] + 0.5 * total_ref[:, :half]
        out_ref[half:, :] = pivot_ref[half:, :] + 0.5 * across.T

    @pl.when(rep != 0)
    def _():
        across = jnp.concatenate([between_ref[...], total_ref[:, half:]], 1)
        out_ref[:half, :] = pivot_ref[:half, :] + 0.5 * across
        out_ref[half:, :] = pivot_ref[half:, :] + 0.5 * total_ref[:, :half]


def call(kernel, shapes, spaces, args, scratch=(), flops=0, room=None):
    vmem = pl.BlockSpec(memory_space=pltpu.VMEM)
    space = {
        "s": pl.BlockSpec(memory_space=pltpu.SMEM),
        "h": pl.BlockSpec(memory_space=pltpu.HBM),
        "v": vmem,
    }
    spaces += "v" * (len(args) - len(spaces))
    moved = sum(4 * a.size for a in args) + sum(4 * functools.reduce(int.__mul__, s) for s in shapes)
    return pl.pallas_call(
        kernel,
        out_shape=[jax.ShapeDtypeStruct(shape, F32) for shape in shapes],
        in_specs=[space[one] for one in spaces],
        out_specs=[vmem] * len(shapes),
        scratch_shapes=[pltpu.VMEM(one, F32) if isinstance(one, tuple) else one for one in scratch],
        compiler_params=pltpu.CompilerParams(vmem_limit_bytes=room or 3 * moved + 2**21),
        cost_estimate=pl.CostEstimate(flops=flops, bytes_accessed=moved, transcendentals=0),
    )(*args)


def body(ancestor_inverse, tile_structure, factor, factor_normalizer, pivot_inverse):
    tile = factor.shape[0]
    half = pivot_inverse.shape[1]
    rows, cols = lax.axis_size("row"), lax.axis_size("col")
    row, col, rep = (lax.axis_index(name) for name in AXES)
    planes, members = cols // PAIR, rows * PAIR
    plane, side = col // PAIR, col % PAIR
    place = jnp.stack([row, plane, side, rep, row * PAIR + side]).astype(jnp.int32)
    depth = rows * tile

    cut = planes // 2
    inner = factor.shape[1]
    own_normed, other_normed, kept, given = call(
        functools.partial(front_kernel, planes, rows),
        [(tile, half), (tile, half), (planes, tile, depth), (cut, tile, depth)],
        "sshhh",
        [place, tile_structure.T, factor, factor_normalizer, ancestor_inverse],
        [
            (tile, inner),
            (PAIR, inner, half),
            (planes, PAIR * tile, depth),
            pltpu.SemaphoreType.DMA((3 + planes,)),
        ],
        room=ROOM,
    )

    def to_plane(r, c, p):
        block = r * cols + c
        peer = block % members
        return peer % rows, block // members * PAIR + peer // rows, p

    def beside(k):
        def target(r, c, p):
            peer = (c % PAIR * rows + r) ^ k
            return peer % rows, c // PAIR * PAIR + peer // rows, p

        return target

    def along(k):
        return lambda r, c, p: (r, c ^ (k * PAIR), p)

    arrived = [send(own_normed, to_plane)]
    arrived += [send(arrived[0], beside(k)) for k in range(1, members)]
    strip = [own_normed] + [send(own_normed, along(k)) for k in range(1, planes)]
    packed = jnp.concatenate(strip[1:], 0)
    other_strip = swap_core(packed)
    mine = send(given, lambda r, c, p: (r, c ^ 1, p))
    theirs = swap_core(mine)
    product, *shares = call(
        functools.partial(product_kernel, planes, members),
        [(planes, tile, half)] + [(tile, half)] * (planes - 1),
        "s",
        [place, kept, mine, theirs, *arrived],
        flops=12 * planes * tile * depth * half,
    )
    other_product = swap_core(product)
    landed = [send(shares[k - 1], along(k)) for k in range(1, planes)]
    ancestor_columns = -(product[0] + sum(landed))

    quarter, step = half // 2, half // members
    width = half + quarter
    parts = call(
        functools.partial(coupling_kernel, members, planes),
        [(step, width)] * members,
        "s",
        [place, product, other_product, other_strip, *strip, other_normed],
        [(half, width)],
        flops=12 * planes * tile * half * half,
    )

    def in_plane(k):
        def target(r, c, p):
            peer = (r * PAIR + c % PAIR) ^ k
            return peer // PAIR, c // PAIR * PAIR + peer % PAIR, p

        return target

    part = parts[0] + sum(send(parts[k], in_plane(k)) for k in range(1, members))
    part = part + sum(send(part, along(k)) for k in range(1, planes))
    parts = [part] + [send(part, in_plane(k)) for k in range(1, members)]
    other_between = swap_core(jnp.concatenate([one[:, half:] for one in parts], 0))
    (diag_block,) = call(
        functools.partial(finish_kernel, members),
        [pivot_inverse.shape],
        "s",
        [place, pivot_inverse, other_between, *parts],
        [(half, width), (half, quarter)],
    )
    return ancestor_columns, diag_block


def solution(mesh):
    return jax.shard_map(
        body,
        mesh=mesh,
        in_specs=(P("row", "col"), P("row", "col"), P(("row", "col"), None), P(), P(None, "rep")),
        out_specs=(P(("row", "col"), "rep"), P(None, "rep")),
        check_vma=False,
    )
```

```python
import functools

import jax
import jax.numpy as jnp
from jax import lax
from jax.experimental import pallas as pl
from jax.experimental.pallas import tpu as pltpu
from jax.sharding import PartitionSpec as P


AXES = ("row", "col", "rep")
PAIR = 2
ROOM_OWN = 56380000
ROOM_MASK = 56000000
F32, BF16 = jnp.float32, jnp.bfloat16


def send(block, target):
    rows, cols, reps = (lax.axis_size(axis) for axis in AXES)

    def flat(r, c, p):
        return (r * cols + c) * reps + p

    route = [
        (flat(r, c, p), flat(*target(r, c, p)))
        for r in range(rows)
        for c in range(cols)
        for p in range(reps)
    ]
    return lax.ppermute(block, AXES, route)


def swap_core(block):
    return send(block, lambda r, c, p: (r, c, 1 - p))


def split(value):
    high = value.astype(BF16)
    return high, (value - high.astype(F32)).astype(BF16)


def split_dot(left, right, contract=(1, 0)):
    dims = (((contract[0],), (contract[1],)), ((), ()))
    product = functools.partial(
        lax.dot_general, dimension_numbers=dims, preferred_element_type=F32
    )
    return (
        product(left[0], right[1]) + product(left[1], right[0]) + product(left[0], right[0])
    )


def tile_at(index, size):
    return pl.ds(pl.multiple_of(index * size, size), size)


def load_all(loads):
    copies = [pltpu.make_async_copy(*load) for load in loads]
    for copy in copies:
        copy.start()
    return copies


def own_kernel(place_ref, factor_ref, normalizer_ref, normed_ref, factor_in, normalizer_in, sems):
    columns = tile_at(place_ref[3], normed_ref.shape[1])
    for copy in load_all(
        [
            (factor_ref, factor_in, sems.at[0]),
            (normalizer_ref.at[:, columns], normalizer_in, sems.at[1]),
        ]
    ):
        copy.wait()
    normed_ref[...] = split_dot(split(factor_in[...]), split(normalizer_in[...]))


def mask_kernel(planes, rows, place_ref, marks_ref, factor_ref, normalizer_ref, full_ref, *refs):
    other_ref, kept_ref, given_ref, factor_in, normalizer_in, full_in, sems = refs
    row, plane, side, rep = (place_ref[i] for i in range(4))
    tile, half = other_ref.shape
    cut = planes // 2
    band = PAIR * tile
    copies = load_all(
        [
            (full_ref.at[tile_at(plane ^ k, band), :], full_in.at[k], sems.at[k])
            for k in range(planes)
        ]
        + [
            (factor_ref, factor_in, sems.at[planes]),
            (normalizer_ref.at[:, tile_at(1 - rep, half)], normalizer_in, sems.at[planes + 1]),
        ]
    )
    for copy in copies[:planes]:
        copy.wait()

    def masked(k, wanted, m):
        across = row ^ m
        mark = marks_ref[across, (plane ^ k) * PAIR + wanted].astype(F32)
        return full_in[k, tile_at(wanted, tile), tile_at(across, tile)] * mark

    for m in range(rows):
        columns = pl.ds(m * tile, tile)

        @pl.loop(0, cut)
        def _(k):
            given_ref[k, :, columns] = masked(k + rep * cut, 1 - side, m)

        @pl.loop(0, planes)
        def _(k):
            kept_ref[k, :, columns] = masked(k, side, m)

    for copy in copies[planes:]:
        copy.wait()
    other_ref[...] = split_dot(split(factor_in[...]), split(normalizer_in[...]))


def product_kernel(planes, members, place_ref, kept_ref, mine_ref, theirs_ref, *refs):
    arrived, outs = refs[:members], refs[members:]
    cut = planes // 2
    rep = place_ref[3]
    right = split(jnp.concatenate([ref[...] for ref in arrived], 0))
    for k in range(planes):
        taken = jnp.where(rep == k // cut, mine_ref[k % cut], theirs_ref[k % cut])
        left = jnp.concatenate([kept_ref[k], taken], 1)
        share = split_dot(split(left), right)
        outs[0][k] = share
        if k:
            outs[k][...] = share


def coupling_kernel(members, planes, place_ref, share_ref, other_ref, gathered_ref, *refs):
    strip, outs, total_ref = refs[: planes + 1], refs[planes + 1 : -1], refs[-1]
    place, first = place_ref[4], place_ref[3] == 0
    tile, half = strip[0].shape
    quarter = half // 2
    step = quarter // members
    own_normed = jnp.concatenate([ref[...] for ref in strip[:planes]], 0)
    other_normed = jnp.concatenate([strip[planes][...], gathered_ref[...]], 0)
    own = share_ref[...].reshape(planes * tile, half)
    other = other_ref[...].reshape(planes * tile, half)
    mixed = split_dot(split(own_normed), split(own), (0, 0))
    lower = mixed[quarter:, :quarter]
    total_ref[:, :quarter] = mixed[:quarter, :quarter] + mixed[:quarter, :quarter].T
    total_ref[:, quarter:half] = mixed[:quarter, quarter:] + lower.T
    total_ref[:, half : half + quarter] = mixed[quarter:, quarter:] + mixed[quarter:, quarter:].T

    def left(mine, theirs):
        return split(jnp.where(first, mine, theirs))

    def right(mine, theirs):
        return split(jnp.where(first, theirs[:, :quarter], mine[:, quarter:]))

    between = split_dot(
        left(own_normed, other_normed), right(own, other), (0, 0)
    ) + split_dot(left(own, other), right(own_normed, other_normed), (0, 0))
    total_ref[:, half + quarter : PAIR * half] = between[:quarter]
    total_ref[:, PAIR * half :] = between[quarter:]
    for k in range(members):
        outs[k][...] = total_ref[tile_at(place ^ k, step), :]


def finish_kernel(members, place_ref, pivot_ref, other_ref, *refs):
    parts, out_ref, total_ref, between_ref = refs[:members], *refs[members:]
    place, rep = place_ref[4], place_ref[3]
    half = out_ref.shape[1]
    quarter = half // 2
    step = quarter // members
    for k in range(members):
        rows = tile_at(place ^ k, step)
        total_ref[rows, :] = parts[k][...]
        between_ref[rows, :] = other_ref[k * step : (k + 1) * step, :]
    blocks = [total_ref[:, i * quarter : (i + 1) * quarter] for i in range(5)]
    others = [between_ref[:, i * quarter : (i + 1) * quarter] for i in range(2)]

    def put(i, j, block):
        at = (pl.ds(i * quarter, quarter), pl.ds(j * quarter, quarter))
        out_ref[at] = pivot_ref[at] + 0.5 * block

    def diagonal(i):
        put(i, 0, blocks[0])
        put(i, 1, blocks[1])
        put(i + 1, 0, blocks[1].T)
        put(i + 1, 1, blocks[2])

    @pl.when(rep == 0)
    def _():
        diagonal(0)
        for i in range(2):
            put(2, i, blocks[3 + i].T)
            put(3, i, others[i].T)

    @pl.when(rep != 0)
    def _():
        diagonal(2)
        for i in range(2):
            put(i, 0, others[i])
            put(i, 1, blocks[3 + i])


def call(kernel, shapes, spaces, args, scratch=(), flops=0, room=None):
    vmem = pl.BlockSpec(memory_space=pltpu.VMEM)
    space = {
        "s": pl.BlockSpec(memory_space=pltpu.SMEM),
        "h": pl.BlockSpec(memory_space=pltpu.HBM),
        "v": vmem,
    }
    spaces += "v" * (len(args) - len(spaces))
    moved = sum(4 * a.size for a in args) + sum(4 * functools.reduce(int.__mul__, s) for s in shapes)
    return pl.pallas_call(
        kernel,
        out_shape=[jax.ShapeDtypeStruct(shape, F32) for shape in shapes],
        in_specs=[space[one] for one in spaces],
        out_specs=[vmem] * len(shapes),
        scratch_shapes=[pltpu.VMEM(one, F32) if isinstance(one, tuple) else one for one in scratch],
        compiler_params=pltpu.CompilerParams(vmem_limit_bytes=room or 3 * moved + 2**21),
        cost_estimate=pl.CostEstimate(flops=flops, bytes_accessed=moved, transcendentals=0),
    )(*args)


def body(ancestor_inverse, tile_structure, factor, factor_normalizer, pivot_inverse):
    tile = factor.shape[0]
    half = pivot_inverse.shape[1]
    rows, cols = lax.axis_size("row"), lax.axis_size("col")
    row, col, rep = (lax.axis_index(name) for name in AXES)
    planes, members = cols // PAIR, rows * PAIR
    plane, side = col // PAIR, col % PAIR
    place = jnp.stack([row, plane, side, rep, row * PAIR + side]).astype(jnp.int32)
    depth = rows * tile

    cut, inner = planes // 2, factor.shape[1]
    inner = factor.shape[1]
    (own_normed,) = call(
        own_kernel,
        [(tile, half)],
        "shh",
        [place, factor, factor_normalizer],
        [(tile, inner), (inner, half), pltpu.SemaphoreType.DMA((2,))],
        room=ROOM_OWN,
    )
    other_normed, kept, given = call(
        functools.partial(mask_kernel, planes, rows),
        [(tile, half), (planes, tile, depth), (cut, tile, depth)],
        "sshhh",
        [place, tile_structure.T, factor, factor_normalizer, ancestor_inverse],
        [
            (tile, inner),
            (inner, half),
            (planes, PAIR * tile, depth),
            pltpu.SemaphoreType.DMA((2 + planes,)),
        ],
        room=ROOM_MASK,
    )

    def to_plane(r, c, p):
        block = r * cols + c
        peer = block % members
        return peer % rows, block // members * PAIR + peer // rows, p

    def beside(k):
        def target(r, c, p):
            peer = (c % PAIR * rows + r) ^ k
            return peer % rows, c // PAIR * PAIR + peer // rows, p

        return target

    def along(k):
        return lambda r, c, p: (r, c ^ (k * PAIR), p)

    arrived = [send(own_normed, to_plane)]
    arrived += [send(arrived[0], beside(k)) for k in range(1, members)]
    strip = [own_normed] + [send(own_normed, along(k)) for k in range(1, planes)]
    packed = jnp.concatenate(strip[1:], 0)
    other_strip = swap_core(packed)
    mine = send(given, lambda r, c, p: (r, c ^ 1, p))
    theirs = swap_core(mine)
    product, *shares = call(
        functools.partial(product_kernel, planes, members),
        [(planes, tile, half)] + [(tile, half)] * (planes - 1),
        "s",
        [place, kept, mine, theirs, *arrived],
        flops=12 * planes * tile * depth * half,
    )
    other_product = swap_core(product)
    landed = [send(shares[k - 1], along(k)) for k in range(1, planes)]
    ancestor_columns = -(product[0] + sum(landed))

    quarter = half // 2
    step, width = quarter // members, 5 * quarter
    parts = call(
        functools.partial(coupling_kernel, members, planes),
        [(step, width)] * members,
        "s",
        [place, product, other_product, other_strip, *strip, other_normed],
        [(quarter, width)],
        flops=12 * planes * tile * half * half,
    )

    def in_plane(k):
        def target(r, c, p):
            peer = (r * PAIR + c % PAIR) ^ k
            return peer // PAIR, c // PAIR * PAIR + peer % PAIR, p

        return target

    part = parts[0] + sum(send(parts[k], in_plane(k)) for k in range(1, members))
    part = part + sum(send(part, along(k)) for k in range(1, planes))
    parts = [part] + [send(part, in_plane(k)) for k in range(1, members)]
    other_between = swap_core(jnp.concatenate([one[:, half + quarter :] for one in parts], 0))
    (diag_block,) = call(
        functools.partial(finish_kernel, members),
        [pivot_inverse.shape],
        "s",
        [place, pivot_inverse, other_between, *parts],
        [(quarter, width), (quarter, half)],
    )
    return ancestor_columns, diag_block


def solution(mesh):
    return jax.shard_map(
        body,
        mesh=mesh,
        in_specs=(P("row", "col"), P("row", "col"), P(("row", "col"), None), P(), P(None, "rep")),
        out_specs=(P(("row", "col"), "rep"), P(None, "rep")),
        check_vma=False,
    )
```

```python
import functools

import jax
import jax.numpy as jnp
from jax import lax
from jax.experimental import pallas as pl
from jax.experimental.pallas import tpu as pltpu
from jax.sharding import PartitionSpec as P


AXES = ("row", "col", "rep")
PAIR = 2
ROOM_OWN = 56380000
ROOM_MASK = 55500000
F32, BF16 = jnp.float32, jnp.bfloat16


def send(block, target):
    rows, cols, reps = (lax.axis_size(axis) for axis in AXES)

    def flat(r, c, p):
        return (r * cols + c) * reps + p

    route = [
        (flat(r, c, p), flat(*target(r, c, p)))
        for r in range(rows)
        for c in range(cols)
        for p in range(reps)
    ]
    return lax.ppermute(block, AXES, route)


def swap_core(block):
    return send(block, lambda r, c, p: (r, c, 1 - p))


def split(value):
    high = value.astype(BF16)
    return high, (value - high.astype(F32)).astype(BF16)


def split_dot(left, right, contract=(1, 0)):
    dims = (((contract[0],), (contract[1],)), ((), ()))
    product = functools.partial(
        lax.dot_general, dimension_numbers=dims, preferred_element_type=F32
    )
    return (
        product(left[0], right[1]) + product(left[1], right[0]) + product(left[0], right[0])
    )


def here():
    return (lax.axis_index(name) for name in AXES)


def tile_at(index, size):
    return pl.ds(pl.multiple_of(index * size, size), size)


def load_all(loads):
    copies = [pltpu.make_async_copy(*load) for load in loads]
    for copy in copies:
        copy.start()
    return copies


def normed_half(other, factor_ref, normalizer_ref, normed_ref, factor_in, normalizer_in, sems):
    rep = lax.axis_index("rep")
    half = normed_ref.shape[1]
    columns = tile_at(1 - rep if other else rep, half)
    chunks, depth = normalizer_in.shape[:2]
    copies = load_all(
        [(factor_ref, factor_in, sems.at[chunks])]
        + [
            (normalizer_ref.at[pl.ds(i * depth, depth), columns], normalizer_in.at[i], sems.at[i])
            for i in range(chunks)
        ]
    )
    total = None
    for i, copy in enumerate(copies):
        copy.wait()
        if i:
            left = factor_in[:, (i - 1) * depth : i * depth]
            term = split_dot(split(left), split(normalizer_in[i - 1]))
            total = term if total is None else total + term
    normed_ref[...] = total


def mask_kernel(planes, rows, marks_ref, full_ref, kept_ref, given_ref, full_in, sems):
    row, col, rep = here()
    plane, side = col // PAIR, col % PAIR
    cut = planes // 2
    tile = kept_ref.shape[1]
    band = PAIR * tile
    copies = load_all(
        [
            (full_ref.at[tile_at(plane ^ k, band), :], full_in.at[k], sems.at[k])
            for k in range(planes)
        ]
    )

    def masked(k, wanted, m):
        across = row ^ m
        mark = marks_ref[across, (plane ^ k) * PAIR + wanted].astype(F32)
        return full_in[k, tile_at(wanted, tile), tile_at(across, tile)] * mark

    for k in range(planes):
        copies[k].wait()
        for m in range(rows):
            kept_ref[k, :, m * tile : (m + 1) * tile] = masked(k, side, m)
    for m in range(rows):

        @pl.loop(0, cut)
        def _(k):
            given_ref[k, :, m * tile : (m + 1) * tile] = masked(k + rep * cut, 1 - side, m)


def product_kernel(planes, members, kept_ref, mine_ref, theirs_ref, *refs):
    arrived, outs = refs[:members], refs[members:]
    cut = planes // 2
    rep = lax.axis_index("rep")
    right = split(jnp.concatenate([ref[...] for ref in arrived], 0))
    for k in range(planes):
        taken = jnp.where(rep == k // cut, mine_ref[k % cut], theirs_ref[k % cut])
        left = jnp.concatenate([kept_ref[k], taken], 1)
        share = split_dot(split(left), right)
        outs[0][k] = share
        if k:
            outs[k][...] = share


def coupling_kernel(members, planes, share_ref, other_ref, gathered_ref, *refs):
    strip, outs, total_ref = refs[: planes + 1], refs[planes + 1 : -1], refs[-1]
    row, col, rep = here()
    place, first = row * PAIR + col % PAIR, rep == 0
    tile, half = strip[0].shape
    quarter = half // 2
    step = quarter // members
    own_normed = jnp.concatenate([ref[...] for ref in strip[:planes]], 0)
    other_normed = jnp.concatenate([strip[planes][...], gathered_ref[...]], 0)
    own = share_ref[...].reshape(planes * tile, half)
    other = other_ref[...].reshape(planes * tile, half)
    mixed = split_dot(split(own_normed), split(own), (0, 0))
    lower = mixed[quarter:, :quarter]
    total_ref[:, :quarter] = mixed[:quarter, :quarter] + mixed[:quarter, :quarter].T
    total_ref[:, quarter:half] = mixed[:quarter, quarter:] + lower.T
    total_ref[:, half : half + quarter] = mixed[quarter:, quarter:] + mixed[quarter:, quarter:].T

    def left(mine, theirs):
        return split(jnp.where(first, mine, theirs))

    def right(mine, theirs):
        return split(jnp.where(first, theirs[:, :quarter], mine[:, quarter:]))

    between = split_dot(
        left(own_normed, other_normed), right(own, other), (0, 0)
    ) + split_dot(left(own, other), right(own_normed, other_normed), (0, 0))
    total_ref[:, half + quarter : PAIR * half] = between[:quarter]
    total_ref[:, PAIR * half :] = between[quarter:]
    for k in range(members):
        outs[k][...] = total_ref[tile_at(place ^ k, step), :]


def finish_kernel(members, pivot_ref, other_ref, *refs):
    parts, out_ref, total_ref, between_ref = refs[:members], *refs[members:]
    row, col, rep = here()
    place = row * PAIR + col % PAIR
    half = out_ref.shape[1]
    quarter = half // 2
    step = quarter // members
    for k in range(members):
        rows = tile_at(place ^ k, step)
        total_ref[rows, :] = parts[k][...]
        between_ref[rows, :] = other_ref[k * step : (k + 1) * step, :]
    blocks = [total_ref[:, i * quarter : (i + 1) * quarter] for i in range(5)]
    others = [between_ref[:, i * quarter : (i + 1) * quarter] for i in range(2)]

    def put(i, j, block):
        at = (pl.ds(i * quarter, quarter), pl.ds(j * quarter, quarter))
        out_ref[at] = pivot_ref[at] + 0.5 * block

    def diagonal(i):
        put(i, 0, blocks[0])
        put(i, 1, blocks[1])
        put(i + 1, 0, blocks[1].T)
        put(i + 1, 1, blocks[2])

    @pl.when(rep == 0)
    def _():
        diagonal(0)
        for i in range(2):
            put(2, i, blocks[3 + i].T)
            put(3, i, others[i].T)

    @pl.when(rep != 0)
    def _():
        diagonal(2)
        for i in range(2):
            put(i, 0, others[i])
            put(i, 1, blocks[3 + i])


def call(kernel, shapes, spaces, args, scratch=(), flops=0, room=None):
    vmem = pl.BlockSpec(memory_space=pltpu.VMEM)
    space = {
        "s": pl.BlockSpec(memory_space=pltpu.SMEM),
        "h": pl.BlockSpec(memory_space=pltpu.HBM),
        "v": vmem,
    }
    spaces += "v" * (len(args) - len(spaces))
    moved = sum(4 * a.size for a in args) + sum(4 * functools.reduce(int.__mul__, s) for s in shapes)
    return pl.pallas_call(
        kernel,
        out_shape=[jax.ShapeDtypeStruct(shape, F32) for shape in shapes],
        in_specs=[space[one] for one in spaces],
        out_specs=[vmem] * len(shapes),
        scratch_shapes=[pltpu.VMEM(one, F32) if isinstance(one, tuple) else one for one in scratch],
        compiler_params=pltpu.CompilerParams(vmem_limit_bytes=room or 3 * moved + 2**21),
        cost_estimate=pl.CostEstimate(flops=flops, bytes_accessed=moved, transcendentals=0),
    )(*args)


def body(ancestor_inverse, tile_structure, factor, factor_normalizer, pivot_inverse):
    tile = factor.shape[0]
    half = pivot_inverse.shape[1]
    rows, cols = lax.axis_size("row"), lax.axis_size("col")
    planes, members = cols // PAIR, rows * PAIR
    depth = rows * tile

    cut, inner = planes // 2, factor.shape[1]
    inner = factor.shape[1]
    chunks = inner // tile

    def normed(other):
        return call(
            functools.partial(normed_half, other),
            [(tile, half)],
            "hh",
            [factor, factor_normalizer],
            [(tile, inner), (chunks, tile, half), pltpu.SemaphoreType.DMA((chunks + 1,))],
            room=ROOM_OWN,
        )[0]

    own_normed = normed(False)
    kept, given = call(
        functools.partial(mask_kernel, planes, rows),
        [(planes, tile, depth), (cut, tile, depth)],
        "sh",
        [tile_structure.T, ancestor_inverse],
        [(planes, PAIR * tile, depth), pltpu.SemaphoreType.DMA((planes,))],
        room=ROOM_MASK,
    )
    other_normed = normed(True)

    def to_plane(r, c, p):
        block = r * cols + c
        peer = block % members
        return peer % rows, block // members * PAIR + peer // rows, p

    def beside(k):
        def target(r, c, p):
            peer = (c % PAIR * rows + r) ^ k
            return peer % rows, c // PAIR * PAIR + peer // rows, p

        return target

    def along(k):
        return lambda r, c, p: (r, c ^ (k * PAIR), p)

    arrived = [send(own_normed, to_plane)]
    arrived += [send(arrived[0], beside(k)) for k in range(1, members)]
    strip = [own_normed] + [send(own_normed, along(k)) for k in range(1, planes)]
    packed = jnp.concatenate(strip[1:], 0)
    other_strip = swap_core(packed)
    mine = send(given, lambda r, c, p: (r, c ^ 1, p))
    theirs = swap_core(mine)
    product, *shares = call(
        functools.partial(product_kernel, planes, members),
        [(planes, tile, half)] + [(tile, half)] * (planes - 1),
        "",
        [kept, mine, theirs, *arrived],
        flops=12 * planes * tile * depth * half,
    )
    other_product = swap_core(product)
    landed = [send(shares[k - 1], along(k)) for k in range(1, planes)]
    ancestor_columns = -(product[0] + sum(landed))

    quarter = half // 2
    step, width = quarter // members, 5 * quarter
    parts = call(
        functools.partial(coupling_kernel, members, planes),
        [(step, width)] * members,
        "",
        [product, other_product, other_strip, *strip, other_normed],
        [(quarter, width)],
        flops=12 * planes * tile * half * half,
    )

    def in_plane(k):
        def target(r, c, p):
            peer = (r * PAIR + c % PAIR) ^ k
            return peer // PAIR, c // PAIR * PAIR + peer % PAIR, p

        return target

    part = parts[0] + sum(send(parts[k], in_plane(k)) for k in range(1, members))
    part = part + sum(send(part, along(k)) for k in range(1, planes))
    parts = [part] + [send(part, in_plane(k)) for k in range(1, members)]
    other_between = swap_core(jnp.concatenate([one[:, half + quarter :] for one in parts], 0))
    (diag_block,) = call(
        functools.partial(finish_kernel, members),
        [pivot_inverse.shape],
        "",
        [pivot_inverse, other_between, *parts],
        [(quarter, width), (quarter, half)],
    )
    return ancestor_columns, diag_block


def solution(mesh):
    return jax.shard_map(
        body,
        mesh=mesh,
        in_specs=(P("row", "col"), P("row", "col"), P(("row", "col"), None), P(), P(None, "rep")),
        out_specs=(P(("row", "col"), "rep"), P(None, "rep")),
        check_vma=False,
    )
```

```python
import functools

import jax
import jax.numpy as jnp
from jax import lax
from jax.experimental import pallas as pl
from jax.experimental.pallas import tpu as pltpu
from jax.sharding import PartitionSpec as P


AXES = ("row", "col", "rep")
PAIR = 2
ROOM_OWN = 56380000
ROOM_MASK = 55500000
F32, BF16 = jnp.float32, jnp.bfloat16


def send(block, target):
    rows, cols, reps = (lax.axis_size(axis) for axis in AXES)

    def flat(r, c, p):
        return (r * cols + c) * reps + p

    route = [
        (flat(r, c, p), flat(*target(r, c, p)))
        for r in range(rows)
        for c in range(cols)
        for p in range(reps)
    ]
    return lax.ppermute(block, AXES, route)


def swap_core(block):
    return send(block, lambda r, c, p: (r, c, 1 - p))


def split(value):
    high = value.astype(BF16)
    return high, (value - high.astype(F32)).astype(BF16)


def split_dot(left, right, contract=(1, 0)):
    dims = (((contract[0],), (contract[1],)), ((), ()))
    product = functools.partial(
        lax.dot_general, dimension_numbers=dims, preferred_element_type=F32
    )
    return (
        product(left[0], right[1]) + product(left[1], right[0]) + product(left[0], right[0])
    )


def here():
    return (lax.axis_index(name) for name in AXES)


def tile_at(index, size):
    return pl.ds(pl.multiple_of(index * size, size), size)


def load_all(loads):
    copies = [pltpu.make_async_copy(*load) for load in loads]
    for copy in copies:
        copy.start()
    return copies


def normed_half(other, factor_ref, normalizer_ref, normed_ref, factor_in, normalizer_in, sems):
    rep = lax.axis_index("rep")
    half = normed_ref.shape[1]
    columns = tile_at(1 - rep if other else rep, half)
    chunks, depth = normalizer_in.shape[:2]
    copies = load_all(
        [(factor_ref, factor_in, sems.at[chunks])]
        + [
            (normalizer_ref.at[pl.ds(i * depth, depth), columns], normalizer_in.at[i], sems.at[i])
            for i in range(chunks)
        ]
    )
    total = None
    for i, copy in enumerate(copies):
        copy.wait()
        if i:
            left = factor_in[:, (i - 1) * depth : i * depth]
            term = split_dot(split(left), split(normalizer_in[i - 1]))
            total = term if total is None else total + term
    normed_ref[...] = total


def mask_kernel(planes, rows, marks_ref, full_ref, kept_ref, given_ref, full_in, sems):
    row, col, rep = here()
    plane, side = col // PAIR, col % PAIR
    cut = planes // 2
    tile = kept_ref.shape[1]
    band = PAIR * tile
    copies = load_all(
        [
            (full_ref.at[tile_at(plane ^ k, band), :], full_in.at[k], sems.at[k])
            for k in range(planes)
        ]
    )

    def masked(k, wanted, m):
        across = row ^ m
        mark = marks_ref[across, (plane ^ k) * PAIR + wanted].astype(F32)
        return full_in[k, tile_at(wanted, tile), tile_at(across, tile)] * mark

    for k in range(planes):
        copies[k].wait()
        for m in range(rows):
            kept_ref[k, :, m * tile : (m + 1) * tile] = masked(k, side, m)
    for m in range(rows):

        @pl.loop(0, cut)
        def _(k):
            given_ref[k, :, m * tile : (m + 1) * tile] = masked(k + rep * cut, 1 - side, m)


def product_kernel(planes, members, kept_ref, mine_ref, theirs_ref, *refs):
    arrived, outs = refs[:members], refs[members:]
    cut = planes // 2
    rep = lax.axis_index("rep")
    right = split(jnp.concatenate([ref[...] for ref in arrived], 0))
    for k in range(planes):
        taken = jnp.where(rep == k // cut, mine_ref[k % cut], theirs_ref[k % cut])
        left = jnp.concatenate([kept_ref[k], taken], 1)
        share = split_dot(split(left), right)
        outs[0][k] = share
        if k % PAIR:
            outs[1][k // PAIR] = share


def coupling_kernel(members, planes, share_ref, other_ref, gathered_ref, *refs):
    strip, outs, total_ref = refs[: planes + 1], refs[planes + 1 : -1], refs[-1]
    row, col, rep = here()
    place, first = row * PAIR + col % PAIR, rep == 0
    tile, half = strip[0].shape
    quarter = half // 2
    step = quarter // members
    own_normed = jnp.concatenate([ref[...] for ref in strip[:planes]], 0)
    other_normed = jnp.concatenate([strip[planes][...], gathered_ref[...]], 0)
    own = share_ref[...].reshape(planes * tile, half)
    other = other_ref[...].reshape(planes * tile, half)
    mixed = split_dot(split(own_normed), split(own), (0, 0))
    lower = mixed[quarter:, :quarter]
    total_ref[:, :quarter] = mixed[:quarter, :quarter] + mixed[:quarter, :quarter].T
    total_ref[:, quarter:half] = mixed[:quarter, quarter:] + lower.T
    total_ref[:, half : half + quarter] = mixed[quarter:, quarter:] + mixed[quarter:, quarter:].T

    def left(mine, theirs):
        return split(jnp.where(first, mine, theirs))

    def right(mine, theirs):
        return split(jnp.where(first, theirs[:, :quarter], mine[:, quarter:]))

    between = split_dot(
        left(own_normed, other_normed), right(own, other), (0, 0)
    ) + split_dot(left(own, other), right(own_normed, other_normed), (0, 0))
    total_ref[:, half + quarter : PAIR * half] = between[:quarter]
    total_ref[:, PAIR * half :] = between[quarter:]
    for k in range(members):
        outs[k][...] = total_ref[tile_at(place ^ k, step), :]


def finish_kernel(members, pivot_ref, other_ref, *refs):
    parts, out_ref, total_ref, between_ref = refs[:members], *refs[members:]
    row, col, rep = here()
    place = row * PAIR + col % PAIR
    half = out_ref.shape[1]
    quarter = half // 2
    step = quarter // members
    for k in range(members):
        rows = tile_at(place ^ k, step)
        total_ref[rows, :] = parts[k][...]
        between_ref[rows, :] = other_ref[k * step : (k + 1) * step, :]
    blocks = [total_ref[:, i * quarter : (i + 1) * quarter] for i in range(5)]
    others = [between_ref[:, i * quarter : (i + 1) * quarter] for i in range(2)]

    def put(i, j, block):
        at = (pl.ds(i * quarter, quarter), pl.ds(j * quarter, quarter))
        out_ref[at] = pivot_ref[at] + 0.5 * block

    def diagonal(i):
        put(i, 0, blocks[0])
        put(i, 1, blocks[1])
        put(i + 1, 0, blocks[1].T)
        put(i + 1, 1, blocks[2])

    @pl.when(rep == 0)
    def _():
        diagonal(0)
        for i in range(2):
            put(2, i, blocks[3 + i].T)
            put(3, i, others[i].T)

    @pl.when(rep != 0)
    def _():
        diagonal(2)
        for i in range(2):
            put(i, 0, others[i])
            put(i, 1, blocks[3 + i])


def call(kernel, shapes, spaces, args, scratch=(), flops=0, room=None):
    vmem = pl.BlockSpec(memory_space=pltpu.VMEM)
    space = {
        "s": pl.BlockSpec(memory_space=pltpu.SMEM),
        "h": pl.BlockSpec(memory_space=pltpu.HBM),
        "v": vmem,
    }
    spaces += "v" * (len(args) - len(spaces))
    moved = sum(4 * a.size for a in args) + sum(4 * functools.reduce(int.__mul__, s) for s in shapes)
    return pl.pallas_call(
        kernel,
        out_shape=[jax.ShapeDtypeStruct(shape, F32) for shape in shapes],
        in_specs=[space[one] for one in spaces],
        out_specs=[vmem] * len(shapes),
        scratch_shapes=[pltpu.VMEM(one, F32) if isinstance(one, tuple) else one for one in scratch],
        compiler_params=pltpu.CompilerParams(vmem_limit_bytes=room or 3 * moved + 2**21),
        cost_estimate=pl.CostEstimate(flops=flops, bytes_accessed=moved, transcendentals=0),
    )(*args)


def body(ancestor_inverse, tile_structure, factor, factor_normalizer, pivot_inverse):
    tile = factor.shape[0]
    half = pivot_inverse.shape[1]
    rows, cols = lax.axis_size("row"), lax.axis_size("col")
    planes, members = cols // PAIR, rows * PAIR
    depth = rows * tile

    cut, inner = planes // 2, factor.shape[1]
    inner = factor.shape[1]
    chunks = inner // tile

    def normed(other):
        return call(
            functools.partial(normed_half, other),
            [(tile, half)],
            "hh",
            [factor, factor_normalizer],
            [(tile, inner), (chunks, tile, half), pltpu.SemaphoreType.DMA((chunks + 1,))],
            room=ROOM_OWN,
        )[0]

    own_normed = normed(False)
    kept, given = call(
        functools.partial(mask_kernel, planes, rows),
        [(planes, tile, depth), (cut, tile, depth)],
        "sh",
        [tile_structure.T, ancestor_inverse],
        [(planes, PAIR * tile, depth), pltpu.SemaphoreType.DMA((planes,))],
        room=ROOM_MASK,
    )
    other_normed = normed(True)

    def to_plane(r, c, p):
        block = r * cols + c
        peer = block % members
        return peer % rows, block // members * PAIR + peer // rows, p

    def beside(k):
        def target(r, c, p):
            peer = (c % PAIR * rows + r) ^ k
            return peer % rows, c // PAIR * PAIR + peer // rows, p

        return target

    def along(k):
        return lambda r, c, p: (r, c ^ (k * PAIR), p)

    arrived = [send(own_normed, to_plane)]
    arrived += [send(arrived[0], beside(k)) for k in range(1, members)]
    strip = [own_normed] + [send(own_normed, along(k)) for k in range(1, planes)]
    packed = jnp.concatenate(strip[1:], 0)
    other_strip = swap_core(packed)
    mine = send(given, lambda r, c, p: (r, c ^ 1, p))
    theirs = swap_core(mine)
    product, given_shares = call(
        functools.partial(product_kernel, planes, members),
        [(planes, tile, half), (planes // PAIR, tile, half)],
        "",
        [kept, mine, theirs, *arrived],
        flops=12 * planes * tile * depth * half,
    )
    other_product = swap_core(product)
    taken_shares = send(given_shares, along(1))
    halved = [product[k] + taken_shares[k // PAIR] for k in range(0, planes, PAIR)]
    landed = [send(halved[k], along(k * PAIR)) for k in range(1, planes // PAIR)]
    ancestor_columns = -(halved[0] + sum(landed))

    quarter = half // 2
    step, width = quarter // members, 5 * quarter
    parts = call(
        functools.partial(coupling_kernel, members, planes),
        [(step, width)] * members,
        "",
        [product, other_product, other_strip, *strip, other_normed],
        [(quarter, width)],
        flops=12 * planes * tile * half * half,
    )

    def in_plane(k):
        def target(r, c, p):
            peer = (r * PAIR + c % PAIR) ^ k
            return peer // PAIR, c // PAIR * PAIR + peer % PAIR, p

        return target

    part = parts[0] + sum(send(parts[k], in_plane(k)) for k in range(1, members))
    part = part + sum(send(part, along(k)) for k in range(1, planes))
    parts = [part] + [send(part, in_plane(k)) for k in range(1, members)]
    other_between = swap_core(jnp.concatenate([one[:, half + quarter :] for one in parts], 0))
    (diag_block,) = call(
        functools.partial(finish_kernel, members),
        [pivot_inverse.shape],
        "",
        [pivot_inverse, other_between, *parts],
        [(quarter, width), (quarter, half)],
    )
    return ancestor_columns, diag_block


def solution(mesh):
    return jax.shard_map(
        body,
        mesh=mesh,
        in_specs=(P("row", "col"), P("row", "col"), P(("row", "col"), None), P(), P(None, "rep")),
        out_specs=(P(("row", "col"), "rep"), P(None, "rep")),
        check_vma=False,
    )
```

```python
import functools

import jax
import jax.numpy as jnp
from jax import lax
from jax.experimental import pallas as pl
from jax.experimental.pallas import tpu as pltpu
from jax.sharding import PartitionSpec as P


AXES = ("row", "col", "rep")
PAIR = 2
ROOM_OWN = 56380000
ROOM_MASK = 55500000
F32, BF16 = jnp.float32, jnp.bfloat16


def send(block, target):
    rows, cols, reps = (lax.axis_size(axis) for axis in AXES)

    def flat(r, c, p):
        return (r * cols + c) * reps + p

    route = [
        (flat(r, c, p), flat(*target(r, c, p)))
        for r in range(rows)
        for c in range(cols)
        for p in range(reps)
    ]
    return lax.ppermute(block, AXES, route)


def swap_core(block):
    return send(block, lambda r, c, p: (r, c, 1 - p))


def split(value):
    high = value.astype(BF16)
    return high, (value - high.astype(F32)).astype(BF16)


def split_dot(left, right, contract=(1, 0)):
    dims = (((contract[0],), (contract[1],)), ((), ()))
    product = functools.partial(
        lax.dot_general, dimension_numbers=dims, preferred_element_type=F32
    )
    return (
        product(left[0], right[1]) + product(left[1], right[0]) + product(left[0], right[0])
    )


def here():
    return (lax.axis_index(name) for name in AXES)


def tile_at(index, size):
    return pl.ds(pl.multiple_of(index * size, size), size)


def load_all(loads):
    copies = [pltpu.make_async_copy(*load) for load in loads]
    for copy in copies:
        copy.start()
    return copies


def normed_half(other, factor_ref, normalizer_ref, normed_ref, factor_in, normalizer_in, sems):
    rep = lax.axis_index("rep")
    half = normed_ref.shape[1]
    columns = tile_at(1 - rep if other else rep, half)
    chunks, depth = normalizer_in.shape[:2]
    copies = load_all(
        [(factor_ref, factor_in, sems.at[chunks])]
        + [
            (normalizer_ref.at[pl.ds(i * depth, depth), columns], normalizer_in.at[i], sems.at[i])
            for i in range(chunks)
        ]
    )
    total = None
    for i, copy in enumerate(copies):
        copy.wait()
        if i:
            left = factor_in[:, (i - 1) * depth : i * depth]
            term = split_dot(split(left), split(normalizer_in[i - 1]))
            total = term if total is None else total + term
    normed_ref[...] = total


def mask_kernel(planes, rows, marks_ref, full_ref, kept_ref, given_ref, full_in, sems):
    row, col, rep = here()
    plane, side = col // PAIR, col % PAIR
    cut = planes // 2
    tile = kept_ref.shape[1]
    band = PAIR * tile
    copies = load_all(
        [
            (full_ref.at[tile_at(plane ^ k, band), :], full_in.at[k], sems.at[k])
            for k in range(planes)
        ]
    )

    def masked(k, wanted, m):
        across = row ^ m
        mark = marks_ref[across, (plane ^ k) * PAIR + wanted].astype(F32)
        return full_in[k, tile_at(wanted, tile), tile_at(across, tile)] * mark

    for k in range(planes):
        copies[k].wait()
        for m in range(rows):
            kept_ref[k, :, m * tile : (m + 1) * tile] = masked(k, side, m)
    for m in range(rows):

        @pl.loop(0, cut)
        def _(k):
            given_ref[k, :, m * tile : (m + 1) * tile] = masked(k + rep * cut, 1 - side, m)


def product_kernel(planes, members, kept_ref, mine_ref, theirs_ref, *refs):
    arrived, outs = refs[:members], refs[members:]
    cut = planes // 2
    rep = lax.axis_index("rep")
    right = split(jnp.concatenate([ref[...] for ref in arrived], 0))
    for k in range(planes):
        taken = jnp.where(rep == k // cut, mine_ref[k % cut], theirs_ref[k % cut])
        left = jnp.concatenate([kept_ref[k], taken], 1)
        share = split_dot(split(left), right)
        outs[0][k] = share
        if k % PAIR:
            outs[1][k // PAIR] = share


def coupling_kernel(members, planes, share_ref, other_ref, *refs):
    strip, other_strip = refs[:planes], refs[planes : 2 * planes]
    outs, total_ref = refs[2 * planes : -1], refs[-1]
    row, col, rep = here()
    place, first = row * PAIR + col % PAIR, rep == 0
    tile, half = strip[0].shape
    quarter = half // 2
    step = quarter // members
    own_normed = jnp.concatenate([ref[...] for ref in strip], 0)
    other_normed = jnp.concatenate([ref[...] for ref in other_strip], 0)
    own = share_ref[...].reshape(planes * tile, half)
    other = other_ref[...].reshape(planes * tile, half)
    mixed = split_dot(split(own_normed), split(own), (0, 0))
    lower = mixed[quarter:, :quarter]
    total_ref[:, :quarter] = mixed[:quarter, :quarter] + mixed[:quarter, :quarter].T
    total_ref[:, quarter:half] = mixed[:quarter, quarter:] + lower.T
    total_ref[:, half : half + quarter] = mixed[quarter:, quarter:] + mixed[quarter:, quarter:].T

    def left(mine, theirs):
        return split(jnp.where(first, mine, theirs))

    def right(mine, theirs):
        return split(jnp.where(first, theirs[:, :quarter], mine[:, quarter:]))

    between = split_dot(
        left(own_normed, other_normed), right(own, other), (0, 0)
    ) + split_dot(left(own, other), right(own_normed, other_normed), (0, 0))
    total_ref[:, half + quarter : PAIR * half] = between[:quarter]
    total_ref[:, PAIR * half :] = between[quarter:]
    for k in range(members):
        outs[k][...] = total_ref[tile_at(place ^ k, step), :]


def finish_kernel(members, pivot_ref, other_ref, *refs):
    parts, out_ref, total_ref, between_ref = refs[:members], *refs[members:]
    row, col, rep = here()
    place = row * PAIR + col % PAIR
    half = out_ref.shape[1]
    quarter = half // 2
    step = quarter // members
    for k in range(members):
        rows = tile_at(place ^ k, step)
        total_ref[rows, :] = parts[k][...]
        between_ref[rows, :] = other_ref[k * step : (k + 1) * step, :]
    blocks = [total_ref[:, i * quarter : (i + 1) * quarter] for i in range(5)]
    others = [between_ref[:, i * quarter : (i + 1) * quarter] for i in range(2)]

    def put(i, j, block):
        at = (pl.ds(i * quarter, quarter), pl.ds(j * quarter, quarter))
        out_ref[at] = pivot_ref[at] + 0.5 * block

    def diagonal(i):
        put(i, 0, blocks[0])
        put(i, 1, blocks[1])
        put(i + 1, 0, blocks[1].T)
        put(i + 1, 1, blocks[2])

    @pl.when(rep == 0)
    def _():
        diagonal(0)
        for i in range(2):
            put(2, i, blocks[3 + i].T)
            put(3, i, others[i].T)

    @pl.when(rep != 0)
    def _():
        diagonal(2)
        for i in range(2):
            put(i, 0, others[i])
            put(i, 1, blocks[3 + i])


def call(kernel, shapes, spaces, args, scratch=(), flops=0, room=None):
    vmem = pl.BlockSpec(memory_space=pltpu.VMEM)
    space = {
        "s": pl.BlockSpec(memory_space=pltpu.SMEM),
        "h": pl.BlockSpec(memory_space=pltpu.HBM),
        "v": vmem,
    }
    spaces += "v" * (len(args) - len(spaces))
    moved = sum(4 * a.size for a in args) + sum(4 * functools.reduce(int.__mul__, s) for s in shapes)
    return pl.pallas_call(
        kernel,
        out_shape=[jax.ShapeDtypeStruct(shape, F32) for shape in shapes],
        in_specs=[space[one] for one in spaces],
        out_specs=[vmem] * len(shapes),
        scratch_shapes=[pltpu.VMEM(one, F32) if isinstance(one, tuple) else one for one in scratch],
        compiler_params=pltpu.CompilerParams(vmem_limit_bytes=room or 3 * moved + 2**21),
        cost_estimate=pl.CostEstimate(flops=flops, bytes_accessed=moved, transcendentals=0),
    )(*args)


def body(ancestor_inverse, tile_structure, factor, factor_normalizer, pivot_inverse):
    tile = factor.shape[0]
    half = pivot_inverse.shape[1]
    rows, cols = lax.axis_size("row"), lax.axis_size("col")
    planes, members = cols // PAIR, rows * PAIR
    depth = rows * tile

    cut, inner = planes // 2, factor.shape[1]
    inner = factor.shape[1]
    chunks = inner // tile

    def normed(other):
        return call(
            functools.partial(normed_half, other),
            [(tile, half)],
            "hh",
            [factor, factor_normalizer],
            [(tile, inner), (chunks, tile, half), pltpu.SemaphoreType.DMA((chunks + 1,))],
            room=ROOM_OWN,
        )[0]

    own_normed = normed(False)
    kept, given = call(
        functools.partial(mask_kernel, planes, rows),
        [(planes, tile, depth), (cut, tile, depth)],
        "sh",
        [tile_structure.T, ancestor_inverse],
        [(planes, PAIR * tile, depth), pltpu.SemaphoreType.DMA((planes,))],
        room=ROOM_MASK,
    )
    other_normed = normed(True)

    def to_plane(r, c, p):
        block = r * cols + c
        peer = block % members
        return peer % rows, block // members * PAIR + peer // rows, p

    def beside(k):
        def target(r, c, p):
            peer = (c % PAIR * rows + r) ^ k
            return peer % rows, c // PAIR * PAIR + peer // rows, p

        return target

    def along(k):
        return lambda r, c, p: (r, c ^ (k * PAIR), p)

    arrived = [send(own_normed, to_plane)]
    arrived += [send(arrived[0], beside(k)) for k in range(1, members)]
    strip = [own_normed] + [send(own_normed, along(k)) for k in range(1, planes)]
    other_strip = [swap_core(strip[k]) for k in range(1, planes)]
    mine = send(given, lambda r, c, p: (r, c ^ 1, p))
    theirs = swap_core(mine)
    product, given_shares = call(
        functools.partial(product_kernel, planes, members),
        [(planes, tile, half), (planes // PAIR, tile, half)],
        "",
        [kept, mine, theirs, *arrived],
        flops=12 * planes * tile * depth * half,
    )
    other_product = swap_core(product)
    taken_shares = send(given_shares, along(1))
    halved = [product[k] + taken_shares[k // PAIR] for k in range(0, planes, PAIR)]
    landed = [send(halved[k], along(k * PAIR)) for k in range(1, planes // PAIR)]
    ancestor_columns = -(halved[0] + sum(landed))

    quarter = half // 2
    step, width = quarter // members, 5 * quarter
    parts = call(
        functools.partial(coupling_kernel, members, planes),
        [(step, width)] * members,
        "",
        [product, other_product, *strip, other_normed, *other_strip],
        [(quarter, width)],
        flops=12 * planes * tile * half * half,
    )

    def in_plane(k):
        def target(r, c, p):
            peer = (r * PAIR + c % PAIR) ^ k
            return peer // PAIR, c // PAIR * PAIR + peer % PAIR, p

        return target

    part = parts[0] + sum(send(parts[k], in_plane(k)) for k in range(1, members))
    part = part + sum(send(part, along(k)) for k in range(1, planes))
    parts = [part] + [send(part, in_plane(k)) for k in range(1, members)]
    other_between = swap_core(jnp.concatenate([one[:, half + quarter :] for one in parts], 0))
    (diag_block,) = call(
        functools.partial(finish_kernel, members),
        [pivot_inverse.shape],
        "",
        [pivot_inverse, other_between, *parts],
        [(quarter, width), (quarter, half)],
    )
    return ancestor_columns, diag_block


def solution(mesh):
    return jax.shard_map(
        body,
        mesh=mesh,
        in_specs=(P("row", "col"), P("row", "col"), P(("row", "col"), None), P(), P(None, "rep")),
        out_specs=(P(("row", "col"), "rep"), P(None, "rep")),
        check_vma=False,
    )
```

```python
import functools

import jax
import jax.numpy as jnp
from jax import lax
from jax.experimental import pallas as pl
from jax.experimental.pallas import tpu as pltpu
from jax.sharding import PartitionSpec as P


AXES = ("row", "col", "rep")
PAIR = 2
SUBLANES = 8
ROOM_OWN = 56380000
ROOM_MASK = 55500000
F32, BF16 = jnp.float32, jnp.bfloat16


def send(block, target):
    rows, cols, reps = (lax.axis_size(axis) for axis in AXES)

    def flat(r, c, p):
        return (r * cols + c) * reps + p

    route = [
        (flat(r, c, p), flat(*target(r, c, p)))
        for r in range(rows)
        for c in range(cols)
        for p in range(reps)
    ]
    return lax.ppermute(block, AXES, route)


def swap_core(block):
    return send(block, lambda r, c, p: (r, c, 1 - p))


def split(value):
    high = value.astype(BF16)
    return high, (value - high.astype(F32)).astype(BF16)


def split_dot(left, right, contract=(1, 0)):
    dims = (((contract[0],), (contract[1],)), ((), ()))
    product = functools.partial(
        lax.dot_general, dimension_numbers=dims, preferred_element_type=F32
    )
    return (
        product(left[0], right[1]) + product(left[1], right[0]) + product(left[0], right[0])
    )


def here():
    return (lax.axis_index(name) for name in AXES)


def tile_at(index, size):
    return pl.ds(pl.multiple_of(index * size, size), size)


def square(size):
    shape = (size, size)
    return lax.broadcasted_iota(jnp.int32, shape, 0), lax.broadcasted_iota(jnp.int32, shape, 1)


def load_all(loads):
    copies = [pltpu.make_async_copy(*load) for load in loads]
    for copy in copies:
        copy.start()
    return copies


def normed_half(other, factor_ref, normalizer_ref, normed_ref, factor_in, normalizer_in, sems):
    rep = lax.axis_index("rep")
    half = normed_ref.shape[1]
    columns = tile_at(1 - rep if other else rep, half)
    chunks, depth = normalizer_in.shape[:2]
    copies = load_all(
        [(factor_ref, factor_in, sems.at[chunks])]
        + [
            (normalizer_ref.at[pl.ds(i * depth, depth), columns], normalizer_in.at[i], sems.at[i])
            for i in range(chunks)
        ]
    )
    total = None
    for i, copy in enumerate(copies):
        copy.wait()
        if i:
            left = factor_in[:, (i - 1) * depth : i * depth]
            term = split_dot(split(left), split(normalizer_in[i - 1]))
            total = term if total is None else total + term
    normed_ref[...] = total


def mask_kernel(planes, rows, marks_ref, full_ref, kept_ref, given_ref, full_in, sems):
    row, col, rep = here()
    plane, side = col // PAIR, col % PAIR
    cut = planes // 2
    tile = kept_ref.shape[1]
    band = PAIR * tile
    copies = load_all(
        [
            (full_ref.at[tile_at(plane ^ k, band), :], full_in.at[k], sems.at[k])
            for k in range(planes)
        ]
    )

    def masked(k, wanted, m):
        across = row ^ m
        mark = marks_ref[across, (plane ^ k) * PAIR + wanted].astype(F32)
        return full_in[k, tile_at(wanted, tile), tile_at(across, tile)] * mark

    for k in range(planes):
        copies[k].wait()
        for m in range(rows):
            kept_ref[k, :, m * tile : (m + 1) * tile] = masked(k, side, m)
    for m in range(rows):

        @pl.loop(0, cut)
        def _(k):
            given_ref[k, :, m * tile : (m + 1) * tile] = masked(k + rep * cut, 1 - side, m)


def product_kernel(planes, members, kept_ref, mine_ref, theirs_ref, *refs):
    arrived, outs = refs[:members], refs[members:]
    cut = planes // 2
    rep = lax.axis_index("rep")
    right = split(jnp.concatenate([ref[...] for ref in arrived], 0))
    for k in range(planes):
        taken = jnp.where(rep == k // cut, mine_ref[k % cut], theirs_ref[k % cut])
        left = jnp.concatenate([kept_ref[k], taken], 1)
        share = split_dot(split(left), right)
        outs[0][k] = share
        if k % PAIR:
            outs[1][k // PAIR] = share


def coupling_kernel(members, planes, share_ref, other_ref, *refs):
    strip, other_strip = refs[:planes], refs[planes : 2 * planes]
    outs, total_ref = refs[2 * planes : -1], refs[-1]
    row, col, rep = here()
    place, first = row * PAIR + col % PAIR, rep == 0
    tile, half = strip[0].shape
    quarter = half // 2
    step = quarter // members
    own_normed = jnp.concatenate([ref[...] for ref in strip], 0)
    other_normed = jnp.concatenate([ref[...] for ref in other_strip], 0)
    own = share_ref[...].reshape(planes * tile, half)
    other = other_ref[...].reshape(planes * tile, half)
    mixed = split_dot(split(own_normed), split(own), (0, 0))
    first_block = mixed[:quarter, :quarter] + mixed[:quarter, :quarter].T
    second_block = mixed[quarter:, quarter:] + mixed[quarter:, quarter:].T
    down, across = square(quarter)
    total_ref[0] = jnp.where(down >= across, first_block, second_block)
    total_ref[1] = mixed[:quarter, quarter:] + mixed[quarter:, :quarter].T
    trace = jnp.sum(jnp.where(down == across, second_block, 0.0), 0, keepdims=True)

    def left(mine, theirs):
        return split(jnp.where(first, mine, theirs))

    def right(mine, theirs):
        return split(jnp.where(first, theirs[:, :quarter], mine[:, quarter:]))

    between = split_dot(
        left(own_normed, other_normed), right(own, other), (0, 0)
    ) + split_dot(left(own, other), right(own_normed, other_normed), (0, 0))
    total_ref[2] = between[:quarter]
    total_ref[3] = between[quarter:]
    down, across = down[:SUBLANES], across[:SUBLANES]
    for k in range(members):
        peer = place ^ k
        for i in range(4):
            outs[k][i * step : (i + 1) * step, :] = total_ref[i, tile_at(peer, step), :]
        inside = (down == 0) & (across >= peer * step) & (across < (peer + 1) * step)
        outs[k][4 * step :, :] = jnp.where(inside, trace, 0.0)


def finish_kernel(members, pivot_ref, other_ref, *refs):
    parts, out_ref, total_ref, between_ref = refs[:members], *refs[members:]
    row, col, rep = here()
    place = row * PAIR + col % PAIR
    half = out_ref.shape[1]
    quarter = half // 2
    step = quarter // members
    trace = parts[0][4 * step : 4 * step + 1, :]
    for k in range(members):
        rows = tile_at(place ^ k, step)
        for i in range(4):
            total_ref[i, rows, :] = parts[k][i * step : (i + 1) * step, :]
        for i in range(2):
            start = (2 * k + i) * step
            between_ref[i, rows, :] = other_ref[start : start + step, :]
        if k:
            trace = trace + parts[k][4 * step : 4 * step + 1, :]
    down, across = square(quarter)
    packed = total_ref[0]
    below, above = (jnp.where(side, packed, 0.0) for side in (down > across, down < across))
    blocks = [
        jnp.where(down == across, packed, below + below.T),
        total_ref[1],
        jnp.where(down == across, trace, above + above.T),
        total_ref[2],
        total_ref[3],
    ]
    others = [between_ref[0], between_ref[1]]

    def put(i, j, block):
        at = (pl.ds(i * quarter, quarter), pl.ds(j * quarter, quarter))
        out_ref[at] = pivot_ref[at] + 0.5 * block

    def diagonal(i):
        put(i, 0, blocks[0])
        put(i, 1, blocks[1])
        put(i + 1, 0, blocks[1].T)
        put(i + 1, 1, blocks[2])

    @pl.when(rep == 0)
    def _():
        diagonal(0)
        for i in range(2):
            put(2, i, blocks[3 + i].T)
            put(3, i, others[i].T)

    @pl.when(rep != 0)
    def _():
        diagonal(2)
        for i in range(2):
            put(i, 0, others[i])
            put(i, 1, blocks[3 + i])


def call(kernel, shapes, spaces, args, scratch=(), flops=0, room=None):
    vmem = pl.BlockSpec(memory_space=pltpu.VMEM)
    space = {
        "s": pl.BlockSpec(memory_space=pltpu.SMEM),
        "h": pl.BlockSpec(memory_space=pltpu.HBM),
        "v": vmem,
    }
    spaces += "v" * (len(args) - len(spaces))
    moved = sum(4 * a.size for a in args) + sum(4 * functools.reduce(int.__mul__, s) for s in shapes)
    return pl.pallas_call(
        kernel,
        out_shape=[jax.ShapeDtypeStruct(shape, F32) for shape in shapes],
        in_specs=[space[one] for one in spaces],
        out_specs=[vmem] * len(shapes),
        scratch_shapes=[pltpu.VMEM(one, F32) if isinstance(one, tuple) else one for one in scratch],
        compiler_params=pltpu.CompilerParams(vmem_limit_bytes=room or 3 * moved + 2**21),
        cost_estimate=pl.CostEstimate(flops=flops, bytes_accessed=moved, transcendentals=0),
    )(*args)


def body(ancestor_inverse, tile_structure, factor, factor_normalizer, pivot_inverse):
    tile = factor.shape[0]
    half = pivot_inverse.shape[1]
    rows, cols = lax.axis_size("row"), lax.axis_size("col")
    planes, members = cols // PAIR, rows * PAIR
    depth = rows * tile

    cut, inner = planes // 2, factor.shape[1]
    inner = factor.shape[1]
    chunks = inner // tile

    def normed(other):
        return call(
            functools.partial(normed_half, other),
            [(tile, half)],
            "hh",
            [factor, factor_normalizer],
            [(tile, inner), (chunks, tile, half), pltpu.SemaphoreType.DMA((chunks + 1,))],
            room=ROOM_OWN,
        )[0]

    own_normed = normed(False)
    kept, given = call(
        functools.partial(mask_kernel, planes, rows),
        [(planes, tile, depth), (cut, tile, depth)],
        "sh",
        [tile_structure.T, ancestor_inverse],
        [(planes, PAIR * tile, depth), pltpu.SemaphoreType.DMA((planes,))],
        room=ROOM_MASK,
    )
    other_normed = normed(True)

    def to_plane(r, c, p):
        block = r * cols + c
        peer = block % members
        return peer % rows, block // members * PAIR + peer // rows, p

    def beside(k):
        def target(r, c, p):
            peer = (c % PAIR * rows + r) ^ k
            return peer % rows, c // PAIR * PAIR + peer // rows, p

        return target

    def along(k):
        return lambda r, c, p: (r, c ^ (k * PAIR), p)

    arrived = [send(own_normed, to_plane)]
    arrived += [send(arrived[0], beside(k)) for k in range(1, members)]
    strip = [own_normed] + [send(own_normed, along(k)) for k in range(1, planes)]
    other_strip = [swap_core(strip[k]) for k in range(1, planes)]
    mine = send(given, lambda r, c, p: (r, c ^ 1, p))
    theirs = swap_core(mine)
    product, given_shares = call(
        functools.partial(product_kernel, planes, members),
        [(planes, tile, half), (planes // PAIR, tile, half)],
        "",
        [kept, mine, theirs, *arrived],
        flops=12 * planes * tile * depth * half,
    )
    other_product = swap_core(product)
    taken_shares = send(given_shares, along(1))
    halved = [product[k] + taken_shares[k // PAIR] for k in range(0, planes, PAIR)]
    landed = [send(halved[k], along(k * PAIR)) for k in range(1, planes // PAIR)]
    ancestor_columns = -(halved[0] + sum(landed))

    quarter = half // 2
    step = quarter // members
    parts = call(
        functools.partial(coupling_kernel, members, planes),
        [(4 * step + SUBLANES, quarter)] * members,
        "",
        [product, other_product, *strip, other_normed, *other_strip],
        [(4, quarter, quarter)],
        flops=12 * planes * tile * half * half,
    )

    def in_plane(k):
        def target(r, c, p):
            peer = (r * PAIR + c % PAIR) ^ k
            return peer // PAIR, c // PAIR * PAIR + peer % PAIR, p

        return target

    part = parts[0] + sum(send(parts[k], in_plane(k)) for k in range(1, members))
    part = part + sum(send(part, along(k)) for k in range(1, planes))
    parts = [part] + [send(part, in_plane(k)) for k in range(1, members)]
    other_between = swap_core(jnp.concatenate([one[2 * step : 4 * step] for one in parts], 0))
    (diag_block,) = call(
        functools.partial(finish_kernel, members),
        [pivot_inverse.shape],
        "",
        [pivot_inverse, other_between, *parts],
        [(4, quarter, quarter), (2, quarter, quarter)],
    )
    return ancestor_columns, diag_block


def solution(mesh):
    return jax.shard_map(
        body,
        mesh=mesh,
        in_specs=(P("row", "col"), P("row", "col"), P(("row", "col"), None), P(), P(None, "rep")),
        out_specs=(P(("row", "col"), "rep"), P(None, "rep")),
        check_vma=False,
    )
```

```python
import functools

import jax
import jax.numpy as jnp
from jax import lax
from jax.experimental import pallas as pl
from jax.experimental.pallas import tpu as pltpu
from jax.sharding import PartitionSpec as P


AXES = ("row", "col", "rep")
PAIR = 2
SUBLANES = 8
ROOM_OWN = 56380000
ROOM_MASK = 55500000
F32, BF16 = jnp.float32, jnp.bfloat16


def send(block, target):
    rows, cols, reps = (lax.axis_size(axis) for axis in AXES)

    def flat(r, c, p):
        return (r * cols + c) * reps + p

    route = [
        (flat(r, c, p), flat(*target(r, c, p)))
        for r in range(rows)
        for c in range(cols)
        for p in range(reps)
    ]
    return lax.ppermute(block, AXES, route)


def swap_core(block):
    return send(block, lambda r, c, p: (r, c, 1 - p))


def split(value):
    high = value.astype(BF16)
    return high, (value - high.astype(F32)).astype(BF16)


def split_dot(left, right, contract=(1, 0)):
    dims = (((contract[0],), (contract[1],)), ((), ()))
    product = functools.partial(
        lax.dot_general, dimension_numbers=dims, preferred_element_type=F32
    )
    return (
        product(left[0], right[1]) + product(left[1], right[0]) + product(left[0], right[0])
    )


def here():
    return (lax.axis_index(name) for name in AXES)


def tile_at(index, size):
    return pl.ds(pl.multiple_of(index * size, size), size)


def square(size):
    shape = (size, size)
    return lax.broadcasted_iota(jnp.int32, shape, 0), lax.broadcasted_iota(jnp.int32, shape, 1)


def load_all(loads):
    copies = [pltpu.make_async_copy(*load) for load in loads]
    for copy in copies:
        copy.start()
    return copies


def normed_half(other, factor_ref, normalizer_ref, normed_ref, factor_in, normalizer_in, sems):
    rep = lax.axis_index("rep")
    half = normed_ref.shape[1]
    columns = tile_at(1 - rep if other else rep, half)
    chunks, depth = normalizer_in.shape[:2]
    copies = load_all(
        [(factor_ref, factor_in, sems.at[chunks])]
        + [
            (normalizer_ref.at[pl.ds(i * depth, depth), columns], normalizer_in.at[i], sems.at[i])
            for i in range(chunks)
        ]
    )
    total = None
    for i, copy in enumerate(copies):
        copy.wait()
        if i:
            left = factor_in[:, (i - 1) * depth : i * depth]
            term = split_dot(split(left), split(normalizer_in[i - 1]))
            total = term if total is None else total + term
    normed_ref[...] = total


def mask_kernel(planes, rows, marks_ref, full_ref, kept_ref, given_ref, full_in, sems):
    row, col, rep = here()
    plane, side = col // PAIR, col % PAIR
    cut = planes // 2
    tile = kept_ref.shape[1]
    band = PAIR * tile
    copies = load_all(
        [
            (full_ref.at[tile_at(plane ^ k, band), :], full_in.at[k], sems.at[k])
            for k in range(planes)
        ]
    )

    def masked(k, wanted, m):
        across = row ^ m
        mark = marks_ref[across, (plane ^ k) * PAIR + wanted].astype(F32)
        return full_in[k, tile_at(wanted, tile), tile_at(across, tile)] * mark

    for k in range(planes):
        copies[k].wait()
        for m in range(rows):
            kept_ref[k, :, m * tile : (m + 1) * tile] = masked(k, side, m)
    for m in range(rows):

        @pl.loop(0, cut)
        def _(k):
            given_ref[k, :, m * tile : (m + 1) * tile] = masked(k + rep * cut, 1 - side, m)


def product_kernel(planes, members, kept_ref, mine_ref, theirs_ref, *refs):
    arrived, outs = refs[:members], refs[members:]
    cut = planes // 2
    rep = lax.axis_index("rep")
    right = split(jnp.concatenate([ref[...] for ref in arrived], 0))
    for k in range(planes):
        taken = jnp.where(rep == k // cut, mine_ref[k % cut], theirs_ref[k % cut])
        left = jnp.concatenate([kept_ref[k], taken], 1)
        share = split_dot(split(left), right)
        outs[0][k] = share
        if k % PAIR:
            outs[1][k // PAIR] = share


def coupling_kernel(members, planes, share_ref, other_ref, *refs):
    strip, other_strip = refs[:planes], refs[planes : 2 * planes]
    outs, total_ref = refs[2 * planes : -1], refs[-1]
    row, col, rep = here()
    place, first = row * PAIR + col % PAIR, rep == 0
    tile, half = strip[0].shape
    quarter = half // 2
    step = quarter // members
    own_normed = jnp.concatenate([ref[...] for ref in strip], 0)
    other_normed = jnp.concatenate([ref[...] for ref in other_strip], 0)
    own = share_ref[...].reshape(planes * tile, half)
    other = other_ref[...].reshape(planes * tile, half)
    mixed = split_dot(split(own_normed), split(own), (0, 0))
    first_block = mixed[:quarter, :quarter] + mixed[:quarter, :quarter].T
    second_block = mixed[quarter:, quarter:] + mixed[quarter:, quarter:].T
    down, across = square(quarter)
    total_ref[0] = jnp.where(down >= across, first_block, second_block)
    total_ref[1] = mixed[:quarter, quarter:] + mixed[quarter:, :quarter].T
    trace = jnp.sum(jnp.where(down == across, second_block, 0.0), 0, keepdims=True)

    def left(mine, theirs):
        return split(jnp.where(first, mine, theirs))

    def right(mine, theirs):
        return split(jnp.where(first, theirs[:, :quarter], mine[:, quarter:]))

    between = split_dot(
        left(own_normed, other_normed), right(own, other), (0, 0)
    ) + split_dot(left(own, other), right(own_normed, other_normed), (0, 0))
    total_ref[2] = between[:quarter]
    total_ref[3] = between[quarter:]
    down, across = down[:SUBLANES], across[:SUBLANES]
    for k in range(members):
        peer = place ^ k
        for i in range(4):
            outs[k][i * step : (i + 1) * step, :] = total_ref[i, tile_at(peer, step), :]
        inside = (down == 0) & (across >= peer * step) & (across < (peer + 1) * step)
        outs[k][4 * step :, :] = jnp.where(inside, trace, 0.0)


def finish_kernel(members, summands, pivot_ref, *refs):
    shares, refs = refs[:summands], refs[summands:]
    parts, pieces = refs[:members], refs[members : 2 * members]
    out_ref, columns_ref, total_ref, between_ref = refs[2 * members :]
    columns_ref[...] = -sum(ref[...] for ref in shares[1:]) - shares[0][...]
    row, col, rep = here()
    place = row * PAIR + col % PAIR
    half = out_ref.shape[1]
    quarter = half // 2
    step = quarter // members
    trace = parts[0][4 * step : 4 * step + 1, :]
    for k in range(members):
        rows = tile_at(place ^ k, step)
        for i in range(4):
            total_ref[i, rows, :] = parts[k][i * step : (i + 1) * step, :]
        for i in range(2):
            between_ref[i, rows, :] = pieces[k][i * step : (i + 1) * step, :]
        if k:
            trace = trace + parts[k][4 * step : 4 * step + 1, :]
    down, across = square(quarter)
    packed = total_ref[0]
    below, above = (jnp.where(side, packed, 0.0) for side in (down > across, down < across))
    blocks = [
        jnp.where(down == across, packed, below + below.T),
        total_ref[1],
        jnp.where(down == across, trace, above + above.T),
        total_ref[2],
        total_ref[3],
    ]
    others = [between_ref[0], between_ref[1]]

    def put(i, j, block):
        at = (pl.ds(i * quarter, quarter), pl.ds(j * quarter, quarter))
        out_ref[at] = pivot_ref[at] + 0.5 * block

    def diagonal(i):
        put(i, 0, blocks[0])
        put(i, 1, blocks[1])
        put(i + 1, 0, blocks[1].T)
        put(i + 1, 1, blocks[2])

    @pl.when(rep == 0)
    def _():
        diagonal(0)
        for i in range(2):
            put(2, i, blocks[3 + i].T)
            put(3, i, others[i].T)

    @pl.when(rep != 0)
    def _():
        diagonal(2)
        for i in range(2):
            put(i, 0, others[i])
            put(i, 1, blocks[3 + i])


def call(kernel, shapes, spaces, args, scratch=(), flops=0, room=None):
    vmem = pl.BlockSpec(memory_space=pltpu.VMEM)
    space = {
        "s": pl.BlockSpec(memory_space=pltpu.SMEM),
        "h": pl.BlockSpec(memory_space=pltpu.HBM),
        "v": vmem,
    }
    spaces += "v" * (len(args) - len(spaces))
    moved = sum(4 * a.size for a in args) + sum(4 * functools.reduce(int.__mul__, s) for s in shapes)
    return pl.pallas_call(
        kernel,
        out_shape=[jax.ShapeDtypeStruct(shape, F32) for shape in shapes],
        in_specs=[space[one] for one in spaces],
        out_specs=[vmem] * len(shapes),
        scratch_shapes=[pltpu.VMEM(one, F32) if isinstance(one, tuple) else one for one in scratch],
        compiler_params=pltpu.CompilerParams(vmem_limit_bytes=room or 3 * moved + 2**21),
        cost_estimate=pl.CostEstimate(flops=flops, bytes_accessed=moved, transcendentals=0),
    )(*args)


def body(ancestor_inverse, tile_structure, factor, factor_normalizer, pivot_inverse):
    tile = factor.shape[0]
    half = pivot_inverse.shape[1]
    rows, cols = lax.axis_size("row"), lax.axis_size("col")
    planes, members = cols // PAIR, rows * PAIR
    depth = rows * tile

    cut, inner = planes // 2, factor.shape[1]
    inner = factor.shape[1]
    chunks = inner // tile

    def normed(other):
        return call(
            functools.partial(normed_half, other),
            [(tile, half)],
            "hh",
            [factor, factor_normalizer],
            [(tile, inner), (chunks, tile, half), pltpu.SemaphoreType.DMA((chunks + 1,))],
            room=ROOM_OWN,
        )[0]

    own_normed = normed(False)
    kept, given = call(
        functools.partial(mask_kernel, planes, rows),
        [(planes, tile, depth), (cut, tile, depth)],
        "sh",
        [tile_structure.T, ancestor_inverse],
        [(planes, PAIR * tile, depth), pltpu.SemaphoreType.DMA((planes,))],
        room=ROOM_MASK,
    )
    other_normed = normed(True)

    def to_plane(r, c, p):
        block = r * cols + c
        peer = block % members
        return peer % rows, block // members * PAIR + peer // rows, p

    def beside(k):
        def target(r, c, p):
            peer = (c % PAIR * rows + r) ^ k
            return peer % rows, c // PAIR * PAIR + peer // rows, p

        return target

    def along(k):
        return lambda r, c, p: (r, c ^ (k * PAIR), p)

    arrived = [send(own_normed, to_plane)]
    arrived += [send(arrived[0], beside(k)) for k in range(1, members)]
    strip = [own_normed] + [send(own_normed, along(k)) for k in range(1, planes)]
    other_strip = [swap_core(strip[k]) for k in range(1, planes)]
    mine = send(given, lambda r, c, p: (r, c ^ 1, p))
    theirs = swap_core(mine)
    product, given_shares = call(
        functools.partial(product_kernel, planes, members),
        [(planes, tile, half), (planes // PAIR, tile, half)],
        "",
        [kept, mine, theirs, *arrived],
        flops=12 * planes * tile * depth * half,
    )
    other_product = swap_core(product)
    taken_shares = send(given_shares, along(1))
    halved = [product[k] + taken_shares[k // PAIR] for k in range(0, planes, PAIR)]
    landed = [send(halved[k], along(k * PAIR)) for k in range(1, planes // PAIR)]
    quarter = half // 2
    step = quarter // members
    parts = call(
        functools.partial(coupling_kernel, members, planes),
        [(4 * step + SUBLANES, quarter)] * members,
        "",
        [product, other_product, *strip, other_normed, *other_strip],
        [(4, quarter, quarter)],
        flops=12 * planes * tile * half * half,
    )

    def in_plane(k):
        def target(r, c, p):
            peer = (r * PAIR + c % PAIR) ^ k
            return peer // PAIR, c // PAIR * PAIR + peer % PAIR, p

        return target

    part = parts[0] + sum(send(parts[k], in_plane(k)) for k in range(1, members))
    part = part + sum(send(part, along(k)) for k in range(1, planes))
    parts = [part] + [send(part, in_plane(k)) for k in range(1, members)]
    pieces = [swap_core(part[2 * step : 4 * step]) for part in parts]
    diag_block, ancestor_columns = call(
        functools.partial(finish_kernel, members, len(landed) + 1),
        [pivot_inverse.shape, (tile, half)],
        "",
        [pivot_inverse, halved[0], *landed, *parts, *pieces],
        [(4, quarter, quarter), (2, quarter, quarter)],
    )
    return ancestor_columns, diag_block


def solution(mesh):
    return jax.shard_map(
        body,
        mesh=mesh,
        in_specs=(P("row", "col"), P("row", "col"), P(("row", "col"), None), P(), P(None, "rep")),
        out_specs=(P(("row", "col"), "rep"), P(None, "rep")),
        check_vma=False,
    )
```

```python
import functools

import jax
import jax.numpy as jnp
from jax import lax
from jax.experimental import pallas as pl
from jax.experimental.pallas import tpu as pltpu
from jax.sharding import PartitionSpec as P


AXES = ("row", "col", "rep")
PAIR = 2
SUBLANES = 8
ROOM_OWN = 56380000
ROOM_MASK = 55500000
F32, BF16 = jnp.float32, jnp.bfloat16


def send(block, target):
    rows, cols, reps = (lax.axis_size(axis) for axis in AXES)

    def flat(r, c, p):
        return (r * cols + c) * reps + p

    route = [
        (flat(r, c, p), flat(*target(r, c, p)))
        for r in range(rows)
        for c in range(cols)
        for p in range(reps)
    ]
    return lax.ppermute(block, AXES, route)


def swap_core(block):
    return send(block, lambda r, c, p: (r, c, 1 - p))


def split(value):
    high = value.astype(BF16)
    return high, (value - high.astype(F32)).astype(BF16)


def split_dot(left, right, contract=(1, 0)):
    dims = (((contract[0],), (contract[1],)), ((), ()))
    product = functools.partial(
        lax.dot_general, dimension_numbers=dims, preferred_element_type=F32
    )
    return (
        product(left[0], right[1]) + product(left[1], right[0]) + product(left[0], right[0])
    )


def here():
    return (lax.axis_index(name) for name in AXES)


def tile_at(index, size):
    return pl.ds(pl.multiple_of(index * size, size), size)


def square(size):
    shape = (size, size)
    return lax.broadcasted_iota(jnp.int32, shape, 0), lax.broadcasted_iota(jnp.int32, shape, 1)


def load_all(loads):
    copies = [pltpu.make_async_copy(*load) for load in loads]
    for copy in copies:
        copy.start()
    return copies


def normed_half(other, factor_ref, normalizer_ref, normed_ref, factor_in, normalizer_in, sems):
    rep = lax.axis_index("rep")
    half = normed_ref.shape[1]
    columns = tile_at(1 - rep if other else rep, half)
    chunks, depth = normalizer_in.shape[:2]
    copies = load_all(
        [(factor_ref, factor_in, sems.at[chunks])]
        + [
            (normalizer_ref.at[pl.ds(i * depth, depth), columns], normalizer_in.at[i], sems.at[i])
            for i in range(chunks)
        ]
    )
    total = None
    for i, copy in enumerate(copies):
        copy.wait()
        if i:
            left = factor_in[:, (i - 1) * depth : i * depth]
            term = split_dot(split(left), split(normalizer_in[i - 1]))
            total = term if total is None else total + term
    normed_ref[...] = total


def mask_kernel(planes, rows, marks_ref, full_ref, kept_ref, given_ref, full_in, sems):
    row, col, rep = here()
    plane, side = col // PAIR, col % PAIR
    cut = planes // 2
    tile = kept_ref.shape[1]
    band = PAIR * tile
    copies = load_all(
        [
            (
                full_ref.at[pl.ds(i * planes * band // 2, planes * band // 2), :],
                full_in.at[pl.ds(i * planes * band // 2, planes * band // 2), :],
                sems.at[i],
            )
            for i in range(2)
        ]
    )
    for copy in copies:
        copy.wait()

    def masked(k, wanted, m):
        across = row ^ m
        mark = marks_ref[across, (plane ^ k) * PAIR + wanted].astype(F32)
        source = (plane ^ k) * PAIR + wanted
        return full_in[tile_at(source, tile), tile_at(across, tile)] * mark

    for k in range(planes):
        for m in range(rows):
            kept_ref[k, :, m * tile : (m + 1) * tile] = masked(k, side, m)
    for k in range(cut):
        for m in range(rows):
            given_ref[k, :, m * tile : (m + 1) * tile] = masked(k + rep * cut, 1 - side, m)


def product_kernel(planes, members, kept_ref, mine_ref, theirs_ref, *refs):
    arrived, outs = refs[:members], refs[members:]
    cut = planes // 2
    rep = lax.axis_index("rep")
    right = split(jnp.concatenate([ref[...] for ref in arrived], 0))
    for k in range(planes):
        taken = jnp.where(rep == k // cut, mine_ref[k % cut], theirs_ref[k % cut])
        left = jnp.concatenate([kept_ref[k], taken], 1)
        share = split_dot(split(left), right)
        outs[0][k] = share
        if k % PAIR:
            outs[1][k // PAIR] = share


def coupling_kernel(members, planes, share_ref, other_ref, *refs):
    strip, other_strip = refs[:planes], refs[planes : 2 * planes]
    outs, total_ref = refs[2 * planes : -1], refs[-1]
    row, col, rep = here()
    place, first = row * PAIR + col % PAIR, rep == 0
    tile, half = strip[0].shape
    quarter = half // 2
    step = quarter // members
    own_normed = jnp.concatenate([ref[...] for ref in strip], 0)
    other_normed = jnp.concatenate([ref[...] for ref in other_strip], 0)
    own = share_ref[...].reshape(planes * tile, half)
    other = other_ref[...].reshape(planes * tile, half)
    mixed = split_dot(split(own_normed), split(own), (0, 0))
    first_block = mixed[:quarter, :quarter] + mixed[:quarter, :quarter].T
    second_block = mixed[quarter:, quarter:] + mixed[quarter:, quarter:].T
    down, across = square(quarter)
    total_ref[0] = jnp.where(down >= across, first_block, second_block)
    total_ref[1] = mixed[:quarter, quarter:] + mixed[quarter:, :quarter].T
    trace = jnp.sum(jnp.where(down == across, second_block, 0.0), 0, keepdims=True)

    def left(mine, theirs):
        return split(jnp.where(first, mine, theirs))

    def right(mine, theirs):
        return split(jnp.where(first, theirs[:, :quarter], mine[:, quarter:]))

    between = split_dot(
        left(own_normed, other_normed), right(own, other), (0, 0)
    ) + split_dot(left(own, other), right(own_normed, other_normed), (0, 0))
    total_ref[2] = between[:quarter]
    total_ref[3] = between[quarter:]
    down, across = down[:SUBLANES], across[:SUBLANES]
    for k in range(members):
        peer = place ^ k
        for i in range(4):
            outs[k][i * step : (i + 1) * step, :] = total_ref[i, tile_at(peer, step), :]
        inside = (down == 0) & (across >= peer * step) & (across < (peer + 1) * step)
        outs[k][4 * step :, :] = jnp.where(inside, trace, 0.0)


def finish_kernel(members, summands, pivot_ref, *refs):
    shares, refs = refs[:summands], refs[summands:]
    parts, pieces = refs[:members], refs[members : 2 * members]
    out_ref, columns_ref, total_ref, between_ref = refs[2 * members :]
    columns_ref[...] = -sum(ref[...] for ref in shares[1:]) - shares[0][...]
    row, col, rep = here()
    place = row * PAIR + col % PAIR
    half = out_ref.shape[1]
    quarter = half // 2
    step = quarter // members
    trace = parts[0][4 * step : 4 * step + 1, :]
    for k in range(members):
        rows = tile_at(place ^ k, step)
        for i in range(4):
            total_ref[i, rows, :] = parts[k][i * step : (i + 1) * step, :]
        for i in range(2):
            between_ref[i, rows, :] = pieces[k][i * step : (i + 1) * step, :]
        if k:
            trace = trace + parts[k][4 * step : 4 * step + 1, :]
    down, across = square(quarter)
    packed = total_ref[0]
    below, above = (jnp.where(side, packed, 0.0) for side in (down > across, down < across))
    blocks = [
        jnp.where(down == across, packed, below + below.T),
        total_ref[1],
        jnp.where(down == across, trace, above + above.T),
        total_ref[2],
        total_ref[3],
    ]
    others = [between_ref[0], between_ref[1]]

    def put(i, j, block):
        at = (pl.ds(i * quarter, quarter), pl.ds(j * quarter, quarter))
        out_ref[at] = pivot_ref[at] + 0.5 * block

    def diagonal(i):
        put(i, 0, blocks[0])
        put(i, 1, blocks[1])
        put(i + 1, 0, blocks[1].T)
        put(i + 1, 1, blocks[2])

    @pl.when(rep == 0)
    def _():
        diagonal(0)
        for i in range(2):
            put(2, i, blocks[3 + i].T)
            put(3, i, others[i].T)

    @pl.when(rep != 0)
    def _():
        diagonal(2)
        for i in range(2):
            put(i, 0, others[i])
            put(i, 1, blocks[3 + i])


def call(kernel, shapes, spaces, args, scratch=(), flops=0, room=None):
    vmem = pl.BlockSpec(memory_space=pltpu.VMEM)
    space = {
        "s": pl.BlockSpec(memory_space=pltpu.SMEM),
        "h": pl.BlockSpec(memory_space=pltpu.HBM),
        "v": vmem,
    }
    spaces += "v" * (len(args) - len(spaces))
    moved = sum(4 * a.size for a in args) + sum(4 * functools.reduce(int.__mul__, s) for s in shapes)
    return pl.pallas_call(
        kernel,
        out_shape=[jax.ShapeDtypeStruct(shape, F32) for shape in shapes],
        in_specs=[space[one] for one in spaces],
        out_specs=[vmem] * len(shapes),
        scratch_shapes=[pltpu.VMEM(one, F32) if isinstance(one, tuple) else one for one in scratch],
        compiler_params=pltpu.CompilerParams(vmem_limit_bytes=room or 3 * moved + 2**21),
        cost_estimate=pl.CostEstimate(flops=flops, bytes_accessed=moved, transcendentals=0),
    )(*args)


def body(ancestor_inverse, tile_structure, factor, factor_normalizer, pivot_inverse):
    tile = factor.shape[0]
    half = pivot_inverse.shape[1]
    rows, cols = lax.axis_size("row"), lax.axis_size("col")
    planes, members = cols // PAIR, rows * PAIR
    depth = rows * tile

    cut, inner = planes // 2, factor.shape[1]
    inner = factor.shape[1]
    chunks = 1

    def normed(other):
        return call(
            functools.partial(normed_half, other),
            [(tile, half)],
            "hh",
            [factor, factor_normalizer],
            [(tile, inner), (chunks, inner // chunks, half), pltpu.SemaphoreType.DMA((chunks + 1,))],
            room=ROOM_OWN,
        )[0]

    own_normed = normed(False)
    kept, given = call(
        functools.partial(mask_kernel, planes, rows),
        [(planes, tile, depth), (cut, tile, depth)],
        "sh",
        [tile_structure.T, ancestor_inverse],
        [(planes * PAIR * tile, depth), pltpu.SemaphoreType.DMA((2,))],
        room=ROOM_MASK,
    )
    other_normed = normed(True)

    def to_plane(r, c, p):
        block = r * cols + c
        peer = block % members
        return peer % rows, block // members * PAIR + peer // rows, p

    def beside(k):
        def target(r, c, p):
            peer = (c % PAIR * rows + r) ^ k
            return peer % rows, c // PAIR * PAIR + peer // rows, p

        return target

    def along(k):
        return lambda r, c, p: (r, c ^ (k * PAIR), p)

    arrived = [send(own_normed, to_plane)]
    arrived += [send(arrived[0], beside(k)) for k in range(1, members)]
    strip = [own_normed] + [send(own_normed, along(k)) for k in range(1, planes)]
    other_strip = [swap_core(strip[k]) for k in range(1, planes)]
    mine = send(given, lambda r, c, p: (r, c ^ 1, p))
    theirs = swap_core(mine)
    product, given_shares = call(
        functools.partial(product_kernel, planes, members),
        [(planes, tile, half), (planes // PAIR, tile, half)],
        "",
        [kept, mine, theirs, *arrived],
        flops=12 * planes * tile * depth * half,
    )
    other_product = swap_core(product)
    taken_shares = send(given_shares, along(1))
    halved = [product[k] + taken_shares[k // PAIR] for k in range(0, planes, PAIR)]
    landed = [send(halved[k], along(k * PAIR)) for k in range(1, planes // PAIR)]
    quarter = half // 2
    step = quarter // members
    parts = call(
        functools.partial(coupling_kernel, members, planes),
        [(4 * step + SUBLANES, quarter)] * members,
        "",
        [product, other_product, *strip, other_normed, *other_strip],
        [(4, quarter, quarter)],
        flops=12 * planes * tile * half * half,
    )

    def in_plane(k):
        def target(r, c, p):
            peer = (r * PAIR + c % PAIR) ^ k
            return peer // PAIR, c // PAIR * PAIR + peer % PAIR, p

        return target

    part = parts[0] + sum(send(parts[k], in_plane(k)) for k in range(1, members))
    part = part + sum(send(part, along(k)) for k in range(1, planes))
    parts = [part] + [send(part, in_plane(k)) for k in range(1, members)]
    pieces = [swap_core(part[2 * step : 4 * step]) for part in parts]
    diag_block, ancestor_columns = call(
        functools.partial(finish_kernel, members, len(landed) + 1),
        [pivot_inverse.shape, (tile, half)],
        "",
        [pivot_inverse, halved[0], *landed, *parts, *pieces],
        [(4, quarter, quarter), (2, quarter, quarter)],
    )
    return ancestor_columns, diag_block


def solution(mesh):
    return jax.shard_map(
        body,
        mesh=mesh,
        in_specs=(P("row", "col"), P("row", "col"), P(("row", "col"), None), P(), P(None, "rep")),
        out_specs=(P(("row", "col"), "rep"), P(None, "rep")),
        check_vma=False,
    )
```
